256 devices in a mesh: slot: 8 (over y, core), asset: 32 (over x, z).
Axes of the slice: x: 4, y: 4, z: 8, core: 2. Of those that a mesh axis runs over, the one named last changes fastest.
Arguments:
- slot_emb: bfloat16 [16384, 768], P(('slot', 'asset')), may hold values from -4 to 4
- asset_panel: bfloat16 [768, 32768], P('slot', 'asset'), may hold values from -4 to 4
- mult: int32 [16384], P('slot'), may hold values from 1 to 4
- caps: int32 [32768], P('asset'), may hold values from 1 to 8, as said below
Outputs:
- plan: float32 [16384, 32768], P('slot', 'asset')
The draws below stay inside these ranges and needn't reach their ends.
Inputs may be any that keep to these rules, and one draw needn't show every extreme that they name: caps are whole numbers; the last asset's cap is the largest.
All inputs are finite; a program needn't handle non-finite values.
Results may differ from the reference program's by a relative error of at most 0.0003.
Values may be sent and summed in bfloat16 or wider, within the bound.
No kernel may reach another device: no remote copies, remote signals or barrier semaphores. Data moves between devices by JAX's collectives and lax.ppermute only.
A program may use at most 64 MiB of HBM per device.

```python
import jax
import jax.numpy as jnp
from jax import lax

EMB = 768
ITERS = 3
SLOTS = 16384
ASSETS = 32768


def base_draw(key, count, width):
    first, second = jax.random.split(key)
    base = jax.random.normal(first, (count, width), jnp.float32)
    scale = jnp.exp(jax.random.uniform(second, (count, 1), jnp.float32, jnp.log(0.5), jnp.log(1.2)))
    return jnp.clip(base * scale, -4.0, 4.0)


def draw_slot_emb(key, part):
    values = base_draw(jax.random.fold_in(key, 1), SLOTS, EMB)
    return values.astype(jnp.bfloat16)


def draw_asset_panel(key, part):
    values = base_draw(jax.random.fold_in(key, 2), ASSETS, EMB)
    return values.T.astype(jnp.bfloat16)


def draw_caps(key, part):
    index = jnp.arange(ASSETS, dtype=jnp.int32)
    upper = 2 + 8 * index // ASSETS
    values = jax.random.randint(jax.random.fold_in(key, 3), (ASSETS,), 1, upper)
    return values.at[ASSETS - 1].set(8).astype(jnp.int32)


def plant(drawn, rng, least, top_value):
    longest = drawn.shape.index(max(drawn.shape))
    spots = []
    for shift in (0, 1):
        where = [jax.random.randint(jax.random.fold_in(rng, axis), (), 0, length) for axis, length in enumerate(drawn.shape)]
        where[longest] = (where[longest] + shift) % drawn.shape[longest]
        spots.append(tuple(where))
    return drawn.at[spots[0]].set(least).at[spots[1]].set(top_value)


def setup_inputs(seed: int = 0) -> dict:
    seeds = jax.random.split(jax.random.key(seed), 5)
    slot_emb = draw_slot_emb(jax.random.fold_in(seeds[4], 71), 0)
    asset_panel = draw_asset_panel(jax.random.fold_in(seeds[4], 71), 0)
    mult = plant(jax.random.randint(seeds[2], (SLOTS,), 1, 5), jax.random.fold_in(seeds[2], 1), 1, 4).astype(jnp.int32)
    caps = draw_caps(jax.random.fold_in(seeds[4], 71), 0)
    return dict(slot_emb=slot_emb, asset_panel=asset_panel, mult=mult, caps=caps)


block_count = 16


def row_lse(logits, asset_pot):
    blocks = logits.reshape(block_count, -1, logits.shape[1])

    def one_block(block):
        return jax.nn.logsumexp(block + asset_pot[None, :], axis=1)

    return lax.map(one_block, blocks).reshape(-1)


def col_lse(logits, slot_pot):
    blocks = logits.reshape(block_count, -1, logits.shape[1])
    pots = slot_pot.reshape(block_count, -1)

    def step(carry, inputs):
        peak, total = carry
        block, pot = inputs
        shifted = block + pot[:, None]
        new_peak = jnp.maximum(peak, jnp.max(shifted, axis=0))
        total = total * jnp.exp(peak - new_peak) + jnp.sum(jnp.exp(shifted - new_peak[None, :]), axis=0)
        return (new_peak, total), None

    init = (jnp.full((logits.shape[1],), -jnp.inf, jnp.float32), jnp.zeros((logits.shape[1],), jnp.float32))
    (peak, total), unused = lax.scan(step, init, (blocks, pots))
    return peak + jnp.log(total)


def reference(slot_emb, asset_panel, mult, caps):
    logits = jnp.dot(slot_emb, asset_panel, preferred_element_type=jnp.float32) * (EMB ** -0.5)
    caps_float = caps.astype(jnp.float32)
    log_b = jnp.log(caps_float) - jnp.log(jnp.sum(caps_float))
    log_a = jnp.log(mult.astype(jnp.float32))
    asset_pot = jnp.zeros((ASSETS,), jnp.float32)
    slot_pot = jnp.zeros((SLOTS,), jnp.float32)
    for iteration in range(ITERS):
        slot_pot = log_a - row_lse(logits, asset_pot)
        asset_pot = log_b - col_lse(logits, slot_pot)
    blocks = logits.reshape(block_count, -1, ASSETS)
    pots = slot_pot.reshape(block_count, -1)
    factor = float(SLOTS * ASSETS)

    def finish(inputs):
        block, pot = inputs
        return jnp.exp(block + pot[:, None] + asset_pot[None, :]) * factor

    return lax.map(finish, (blocks, pots)).reshape(SLOTS, ASSETS)
```

```python
import jax
import jax.numpy as jnp
from jax import lax
from jax.sharding import Mesh, PartitionSpec as P

EMB = 768
ITERS = 3


def shift(value, axis, step):
    size = lax.axis_size(axis)
    return lax.ppermute(value, axis, [(i, (i + step) % size) for i in range(size)])


def ring_gather(value, axis):
    size = lax.axis_size(axis)
    shards = [None] * size
    shards[0] = value
    ahead = behind = value
    for step in range(1, size // 2):
        ahead = shift(ahead, axis, 1)
        behind = shift(behind, axis, -1)
        shards[step] = ahead
        shards[size - step] = behind
    half = value.shape[0] // 2
    shards[size // 2] = jnp.concatenate(
        [shift(ahead[:half], axis, 1), shift(behind[half:], axis, -1)]
    )
    return shards


def in_order(shards, axis):
    size = lax.axis_size(axis)
    me = lax.axis_index(axis)
    backward = jnp.stack([shards[(-k) % size] for k in range(size)])
    twice = jnp.concatenate([backward, backward])
    return lax.dynamic_slice_in_dim(twice, (size - me) % size, size, axis=0)


def spread(value, axes, size):
    copies = jnp.broadcast_to(value[None], (size,) + value.shape)
    return lax.all_to_all(copies, axes, 0, 0, tiled=True)


def lse(parts):
    peak = jnp.max(parts, axis=0)
    return peak + jnp.log(jnp.sum(jnp.exp(parts - peak[None]), axis=0))


def over_slot(value):
    value = value + shift(value, "c", 1)
    return value + shift(value, "y", 1) + shift(value, "y", 2) + shift(value, "y", -1)


def per_device(slot_emb, asset_panel, mult, caps):
    half = EMB // 2
    first = jnp.stack(ring_gather(slot_emb[:, :half], "x"))
    second = jnp.stack(ring_gather(slot_emb[:, half:], "z"))
    panel = jnp.stack(ring_gather(asset_panel, "y"))
    other = shift(panel, "c", 1)
    first = jnp.stack(ring_gather(first, "z"))
    second = jnp.stack(ring_gather(second, "x"))
    first = in_order([in_order([first[k, j] for j in range(4)], "x") for k in range(8)], "z")
    second = in_order([in_order([second[j, k] for k in range(8)], "z") for j in range(4)], "x")
    rows = 2048
    first = jnp.swapaxes(first, 0, 1).reshape(rows, half)
    second = second.reshape(rows, half)
    panel = in_order([panel[k] for k in range(4)], "y")
    other = in_order([other[k] for k in range(4)], "y")
    core = lax.axis_index("c")
    low = jnp.where(core == 0, panel, other)
    high = jnp.where(core == 0, other, panel)
    panel = jnp.stack([low, high], axis=1).reshape(EMB, -1)
    logits = (
        jnp.dot(first, panel[:half], preferred_element_type=jnp.float32)
        + jnp.dot(second, panel[half:], preferred_element_type=jnp.float32)
    ) * EMB ** (-0.5)
    caps_float = caps.astype(jnp.float32)
    cap_total = jnp.sum(spread(jnp.full((8, 128), jnp.sum(caps_float)), ("x", "z"), 32)[:, 0, 0])
    share = caps_float / cap_total
    log_b = jnp.log(caps_float) - jnp.log(cap_total)
    weight = mult.astype(jnp.float32)
    log_a = jnp.log(weight)

    peak = jnp.max(logits, axis=1)
    part = peak + jnp.log(jnp.sum(jnp.exp(logits - peak[:, None]), axis=1))
    slot_pot = log_a - lse(spread(part.reshape(16, 128), ("x", "z"), 32)).reshape(-1)
    shifted = logits + slot_pot[:, None]
    peak = jnp.max(shifted, axis=0)
    part = peak + jnp.log(jnp.sum(jnp.exp(shifted - peak[None, :]), axis=0))
    asset_pot = log_b - lse(spread(part.reshape(8, 128), ("y", "c"), 8)).reshape(-1)

    scaled = jnp.exp(logits + slot_pot[:, None] + asset_pot[None, :])
    v = jnp.ones_like(share)
    for iteration in range(1, ITERS):
        part = jnp.sum(scaled * v[None, :], axis=1)
        u = weight / jnp.sum(spread(part.reshape(16, 128), ("x", "z"), 32), axis=0).reshape(-1)
        v = share / over_slot(jnp.sum(scaled * u[:, None], axis=0).reshape(8, 128)).reshape(-1)
    factor = float(16384 * 32768)
    return scaled * u[:, None] * (v * factor)[None, :]


def solution(mesh):
    fine = Mesh(mesh.devices.reshape(4, 2, 4, 8), ("y", "c", "x", "z"))
    slot, asset = ("y", "c"), ("x", "z")
    return jax.shard_map(
        per_device,
        mesh=fine,
        in_specs=(P(slot + asset, None), P(slot, asset), P(slot), P(asset)),
        out_specs=P(slot, asset),
        check_vma=False,
    )
```

```python
import functools

import jax
import jax.numpy as jnp
from jax import lax
from jax.experimental import pallas as pl
from jax.experimental.pallas import tpu as pltpu
from jax.sharding import Mesh, PartitionSpec as P

EMB = 768
ITERS = 3
SLOTS = 16384
ASSETS = 32768
ROWS, COLS = 2048, 1024
LANES, SUB = 128, 8
RB, CB = ROWS // LANES, COLS // LANES
VMEM_LIMIT = 28 << 20
F32 = jnp.float32


def shift(value, axis, step):
    size = lax.axis_size(axis)
    return lax.ppermute(value, axis, [(i, (i + step) % size) for i in range(size)])


def ring_gather(value, axis):
    size = lax.axis_size(axis)
    shards = {0: [value]}
    ahead = behind = value
    for step in range(1, size // 2):
        ahead = shift(ahead, axis, 1)
        behind = shift(behind, axis, -1)
        shards[step] = [ahead]
        shards[size - step] = [behind]
    half = value.shape[0] // 2
    shards[size // 2] = [shift(ahead[:half], axis, 1), shift(behind[half:], axis, -1)]
    return shards


def whole(pieces):
    return pieces[0] if len(pieces) == 1 else jnp.concatenate(pieces)


def over_asset(part):
    copies = jnp.broadcast_to(part[None], (32,) + part.shape)
    return lax.all_to_all(copies, ("x", "z"), 0, 0, tiled=True)


def over_slot(part, combine):
    part = combine(part, shift(part, "c", 1))
    return [part] + [shift(part, "y", step) for step in (2, 1, -1)]


def iotas():
    lane = lax.broadcasted_iota(jnp.int32, (SUB, LANES), 1)
    row = lax.broadcasted_iota(jnp.int32, (SUB, LANES), 0)
    return lane, row


def column(row, g):
    lane, sub = iotas()
    return jnp.sum(jnp.where(lane == sub + SUB * g, row, 0.0), axis=1, keepdims=True)


def place(acc, col, g):
    lane, sub = iotas()
    return jnp.where(lane == sub + SUB * g, col, acc)


def long_row(dense):
    row = jnp.concatenate([dense[k : k + 1, :] for k in range(CB)], axis=1)
    return jnp.broadcast_to(row, (SUB, COLS))


def put_dense(ref, row):
    for k in range(CB):
        ref[k : k + 1, :] = row[:, LANES * k : LANES * (k + 1)]


def fold(wide):
    total = wide[:, :LANES]
    for k in range(1, CB):
        total = total + wide[:, LANES * k : LANES * (k + 1)]
    return total


def log_sum(parts):
    peak = functools.reduce(jnp.maximum, parts)
    return peak + jnp.log(functools.reduce(jnp.add, [jnp.exp(p - peak) for p in parts]))


def groups(b):
    for g in range(LANES // SUB):
        yield g, pl.ds(pl.multiple_of(b * LANES + SUB * g, SUB), SUB)


def logits_kernel(plan, *refs):
    count = len(plan)
    pieces, (logits, part), (slot, panel, sems) = refs[:count], refs[count : count + 2], refs[count + 2 :]
    place_of = {a: lax.axis_index(a) for a in ("y", "c", "x", "z")}
    size_of = {"y": 4, "c": 2, "x": 4, "z": 8}
    copies = []
    for piece, blocks in zip(pieces, plan):
        for kind, at, back, offset, rows in blocks:
            pos = {a: lax.rem(place_of[a] - k + size_of[a], size_of[a]) for a, k in back.items()}
            if kind == "slot":
                start = (pos["x"] * 8 + pos["z"]) * 64 + offset
                target = slot
            else:
                start = (pos["y"] * 2 + pos["c"]) * 96 + offset
                target = panel
            copies.append(
                pltpu.make_async_copy(
                    piece.at[pl.ds(at, rows)],
                    target.at[pl.ds(pl.multiple_of(start, 16), rows)],
                    sems.at[len(copies)],
                )
            )
    for copy in copies:
        copy.start()
    for copy in copies:
        copy.wait()

    def block(b, carry):
        rows = pl.ds(pl.multiple_of(b * LANES, LANES), LANES)
        logits[rows, :] = jnp.dot(slot[rows, :], panel[...], preferred_element_type=F32) * EMB ** (-0.5)
        peaks = jnp.zeros((SUB, LANES), F32)
        totals = jnp.zeros((SUB, LANES), F32)
        for g, at in groups(b):
            x = logits[at, :]
            peak = jnp.max(x, axis=1, keepdims=True)
            total = jnp.sum(fold(jnp.exp(x - peak)), axis=1, keepdims=True)
            peaks = place(peaks, peak, g)
            totals = place(totals, total, g)
        peaks = jnp.sum(peaks, axis=0, keepdims=True)
        totals = jnp.sum(totals, axis=0, keepdims=True)
        part[pl.ds(b, 1), :] = peaks + jnp.log(totals)
        return carry

    lax.fori_loop(0, RB, block, 0)


def first_col_kernel(logits, parts, mult, shifted, part, pot):
    peak = jnp.max(parts[...], axis=0)
    lse = peak + jnp.log(jnp.sum(jnp.exp(parts[...] - peak[None]), axis=0))
    pot[...] = jnp.log(mult[...].astype(F32)) - lse

    def block(b, carry):
        top, total = carry
        row = pot[pl.ds(b, 1), :]
        new = top
        for g, at in groups(b):
            x = logits[at, :] + column(row, g)
            shifted[at, :] = x
            new = jnp.maximum(new, x)
        total = total * jnp.exp(top - new)
        for g, at in groups(b):
            total = total + jnp.exp(shifted[at, :] - new)
        return new, total

    start = (jnp.full((SUB, COLS), -jnp.inf, F32), jnp.zeros((SUB, COLS), F32))
    top, total = lax.fori_loop(0, RB, block, start)
    peak = jnp.max(top, axis=0, keepdims=True)
    total = jnp.sum(total * jnp.exp(top - peak), axis=0, keepdims=True)
    put_dense(part, peak + jnp.log(total))


def scale_kernel(shifted, a, b, c, d, caps, scaled, part):
    lse = log_sum([a[...], b[...], c[...], d[...]])
    pot = long_row(jnp.log(caps[...].astype(F32)) - lse)

    def block(b, carry):
        acc = jnp.zeros((SUB, LANES), F32)
        for g, at in groups(b):
            x = jnp.exp(shifted[at, :] + pot)
            scaled[at, :] = x
            acc = place(acc, jnp.sum(fold(x), axis=1, keepdims=True), g)
        part[pl.ds(b, 1), :] = jnp.sum(acc, axis=0, keepdims=True)
        return carry

    lax.fori_loop(0, RB, block, 0)


def col_kernel(scaled, parts, mult, part, u):
    u[...] = mult[...].astype(F32) / jnp.sum(parts[:, :RB, :], axis=0)

    def block(b, total):
        row = u[pl.ds(b, 1), :]
        for g, at in groups(b):
            total = total + scaled[at, :] * column(row, g)
        return total

    total = lax.fori_loop(0, RB, block, jnp.zeros((SUB, COLS), F32))
    put_dense(part, jnp.sum(total, axis=0, keepdims=True))


def row_kernel(scaled, a, b, c, d, caps, part):
    caps_float = caps[...].astype(F32)
    v = long_row(caps_float / (a[...] + b[...] + c[...] + d[...]))

    def block(b, carry):
        acc = jnp.zeros((SUB, LANES), F32)
        for g, at in groups(b):
            acc = place(acc, jnp.sum(fold(scaled[at, :] * v), axis=1, keepdims=True), g)
        part[pl.ds(b, 1), :] = jnp.sum(acc, axis=0, keepdims=True)
        return carry

    lax.fori_loop(0, RB, block, 0)
    part[RB:, :] = jnp.broadcast_to(jnp.sum(caps_float), (SUB, LANES))


def plan_kernel(scaled, u, a, b, c, d, caps, parts, plan):
    step = pl.program_id(0)
    cap_total = jnp.sum(parts[:, RB:, :], axis=0)
    v = caps[...].astype(F32) / (a[...] + b[...] + c[...] + d[...])
    v = long_row(v * (float(SLOTS * ASSETS) / cap_total))
    for half in range(2):
        row = u[pl.ds(step * 2 + half, 1), :]
        for g in range(LANES // SUB):
            at = pl.ds(pl.multiple_of(step * 256 + half * LANES + SUB * g, SUB), SUB)
            plan[half * LANES + SUB * g : half * LANES + SUB * (g + 1), :] = scaled[at, :] * column(row, g) * v


def call(kernel, out_shape, scratch=(), **kwargs):
    return pl.pallas_call(
        kernel,
        out_shape=out_shape,
        scratch_shapes=list(scratch),
        compiler_params=pltpu.CompilerParams(vmem_limit_bytes=VMEM_LIMIT),
        **kwargs,
    )


def in_vmem(value):
    return pltpu.with_memory_space_constraint(value, pltpu.VMEM)


VM = pl.BlockSpec(memory_space=pltpu.VMEM)


def small(rows):
    return jax.ShapeDtypeStruct((rows, LANES), F32)


def per_device(slot_emb, asset_panel, mult, caps):
    mult = mult.reshape(RB, LANES)
    caps = caps.reshape(CB, LANES)

    first = ring_gather(slot_emb[:32], "x")
    second = ring_gather(slot_emb[32:], "z")
    panel = ring_gather(asset_panel, "y")
    first = ring_gather(jnp.concatenate([whole(first[j]) for j in range(4)]), "z")
    second = ring_gather(jnp.concatenate([whole(second[k]) for k in range(8)]), "x")
    pieces, plan = [], []
    for k in range(8):
        j = 0
        for piece in first[k]:
            blocks = []
            for at in range(0, piece.shape[0], 32):
                blocks.append(("slot", at, {"x": j, "z": k}, 0, 32))
                j += 1
            pieces.append(piece)
            plan.append(blocks)
    for j in range(4):
        k = 0
        for piece in second[j]:
            blocks = []
            for at in range(0, piece.shape[0], 32):
                blocks.append(("slot", at, {"x": j, "z": k}, 32, 32))
                k += 1
            pieces.append(piece)
            plan.append(blocks)
    for k in range(4):
        offset = 0
        for piece in panel[k]:
            rows = piece.shape[0]
            pieces += [piece, shift(piece, "c", 1)]
            plan += [[("panel", 0, {"y": k, "c": j}, offset, rows)] for j in range(2)]
            offset += rows
    block = pltpu.VMEM((ROWS, COLS), F32)
    logits, part = call(
        functools.partial(logits_kernel, plan),
        (block, small(RB)),
        in_specs=[pl.BlockSpec(memory_space=pl.ANY)] * len(pieces),
        out_specs=(VM, VM),
        scratch=[
            pltpu.VMEM((ROWS, EMB), jnp.bfloat16),
            pltpu.VMEM((EMB, COLS), jnp.bfloat16),
            pltpu.SemaphoreType.DMA((sum(map(len, plan)),)),
        ],
    )(*pieces)

    shifted, part = call(
        first_col_kernel, (block, small(CB)), in_specs=[VM] * 3, out_specs=(VM, VM),
        scratch=[pltpu.VMEM((RB, LANES), F32)],
    )(in_vmem(logits), over_asset(part), mult)
    parts = over_slot(part, jnp.logaddexp)

    scaled, part = call(scale_kernel, (block, small(RB)), in_specs=[VM] * 6, out_specs=(VM, VM))(
        in_vmem(shifted), *parts, caps
    )
    for iteration in range(1, ITERS):
        row_parts = over_asset(part)
        part, u = call(col_kernel, (small(CB), small(RB)), in_specs=[VM] * 3, out_specs=(VM, VM))(
            in_vmem(scaled), row_parts, mult
        )
        parts = over_slot(part, jnp.add)
        if iteration < ITERS - 1:
            part = call(row_kernel, small(RB + SUB), in_specs=[VM] * 6, out_specs=VM)(in_vmem(scaled), *parts, caps)
    return call(
        plan_kernel,
        jax.ShapeDtypeStruct((ROWS, COLS), F32),
        grid=(ROWS // 256,),
        in_specs=[VM] * 8,
        out_specs=pl.BlockSpec((256, COLS), lambda i: (i, 0)),
    )(in_vmem(scaled), u, *parts, caps, row_parts)


def solution(mesh):
    fine = Mesh(mesh.devices.reshape(4, 2, 4, 8), ("y", "c", "x", "z"))
    slot, asset = ("y", "c"), ("x", "z")
    return jax.shard_map(
        per_device,
        mesh=fine,
        in_specs=(P(slot + asset, None), P(slot, asset), P(slot), P(asset)),
        out_specs=P(slot, asset),
        check_vma=False,
    )
```

```python
import functools

import jax
import jax.numpy as jnp
from jax import lax
from jax.experimental import pallas as pl
from jax.experimental.pallas import tpu as pltpu
from jax.sharding import Mesh, PartitionSpec as P

EMB = 768
ITERS = 3
SLOTS = 16384
ASSETS = 32768
ROWS, COLS = 2048, 1024
LANES, SUB = 128, 8
RB, CB = ROWS // LANES, COLS // LANES
VMEM_LIMIT = 28 << 20
BLOCK = 512
F32 = jnp.float32


def shift(value, axis, step):
    size = lax.axis_size(axis)
    return lax.ppermute(value, axis, [(i, (i + step) % size) for i in range(size)])


def ring_gather(value, axis):
    size = lax.axis_size(axis)
    shards = {0: [value]}
    ahead = behind = value
    for step in range(1, size // 2):
        ahead = shift(ahead, axis, 1)
        behind = shift(behind, axis, -1)
        shards[step] = [ahead]
        shards[size - step] = [behind]
    half = value.shape[0] // 2
    shards[size // 2] = [shift(ahead[:half], axis, 1), shift(behind[half:], axis, -1)]
    return shards


def over_asset(part):
    copies = jnp.broadcast_to(part[None], (32,) + part.shape)
    return lax.all_to_all(copies, ("x", "z"), 0, 0, tiled=True)


def over_slot(part):
    copies = jnp.broadcast_to(part[None], (8,) + part.shape)
    return lax.all_to_all(copies, ("y", "c"), 0, 0, tiled=True)


def iotas():
    lane = lax.broadcasted_iota(jnp.int32, (SUB, LANES), 1)
    row = lax.broadcasted_iota(jnp.int32, (SUB, LANES), 0)
    return lane, row


def column(row, g):
    lane, sub = iotas()
    return jnp.sum(jnp.where(lane == sub + SUB * g, row, 0.0), axis=1, keepdims=True)


def place(acc, col, g):
    lane, sub = iotas()
    return jnp.where(lane == sub + SUB * g, col, acc)


def long_row(dense):
    row = jnp.concatenate([dense[k : k + 1, :] for k in range(CB)], axis=1)
    return jnp.broadcast_to(row, (SUB, COLS))


def put_dense(ref, row):
    for k in range(CB):
        ref[k : k + 1, :] = row[:, LANES * k : LANES * (k + 1)]


def fold(wide):
    total = wide[:, :LANES]
    for k in range(1, CB):
        total = total + wide[:, LANES * k : LANES * (k + 1)]
    return total


def log_sum(parts):
    peak = jnp.max(parts, axis=0)
    return peak + jnp.log(jnp.sum(jnp.exp(parts - peak[None]), axis=0))


def groups(b):
    for g in range(LANES // SUB):
        yield g, pl.ds(pl.multiple_of(b * LANES + SUB * g, SUB), SUB)


def row_stats(logits, part, unit):
    peaks = []
    for g, at in groups(unit):
        x = logits[at, :]
        wide = x[:, :LANES]
        for k in range(1, CB):
            wide = jnp.maximum(wide, x[:, LANES * k : LANES * (k + 1)])
        peaks.append(jnp.max(wide, axis=1, keepdims=True))
    totals = []
    for g, at in groups(unit):
        totals.append(jnp.sum(fold(jnp.exp(logits[at, :] - peaks[g])), axis=1, keepdims=True))
    peak_row = jnp.zeros((SUB, LANES), F32)
    total_row = jnp.zeros((SUB, LANES), F32)
    for g in range(LANES // SUB):
        peak_row = place(peak_row, peaks[g], g)
        total_row = place(total_row, totals[g], g)
    peak_row = jnp.sum(peak_row, axis=0, keepdims=True)
    part[pl.ds(unit, 1), :] = peak_row + jnp.log(jnp.sum(total_row, axis=0, keepdims=True))


def block_logits(slot, panel, logits, part, table, count):
    def block(b, carry):
        rows = pl.ds(pl.multiple_of(b * BLOCK, BLOCK), BLOCK)
        value = jnp.dot(slot[rows, :], panel[...], preferred_element_type=F32) * EMB ** (-0.5)
        units = BLOCK // LANES
        for t in range(units):
            at = pl.ds(pl.multiple_of(table[b * units + t] * LANES, LANES), LANES)
            logits[at, :] = value[LANES * t : LANES * (t + 1), :]

        def stats(t, carry):
            row_stats(logits, part, table[b * units + t])
            return carry

        return lax.fori_loop(0, units, stats, carry)

    lax.fori_loop(0, count // BLOCK, block, 0)


def back(axis, steps):
    size = lax.axis_size(axis)
    return lax.rem(lax.axis_index(axis) - steps + size, size)


def put_slots(pieces, names, slot, table):
    at = unit = 0
    for ref, (axis, steps, offset) in zip(pieces, names):
        rows = ref.shape[0]
        slot[at : at + rows, :] = ref[...]
        at += rows
        first = back("z", steps) if axis == "z" else 8 + 2 * back("x", steps) + offset
        for i in range(rows // LANES):
            table[unit] = first + i
            unit += 1


def early_kernel(panel_names, slot_names, *refs):
    n, m = len(panel_names), len(slot_names)
    panels, slots = refs[:n], refs[n : n + m]
    logits, part, panel, slot, table = refs[n + m :]
    for ref, (y_steps, c_steps) in zip(panels, panel_names):
        start = (back("y", y_steps) * 2 + back("c", c_steps)) * 96
        panel[pl.ds(pl.multiple_of(start, 16), 96), :] = ref[...]
    put_slots(slots, slot_names, slot, table)
    block_logits(slot, panel, logits, part, table, slot.shape[0])


def late_kernel(*refs):
    before, part_before, panel, a5, a4, b4, c0, c1, logits, part, slot, table = refs
    del before, part_before
    slot[:LANES, :] = a5[...]
    slot[LANES : LANES + 64, :] = a4[...]
    slot[LANES + 64 : 2 * LANES, :] = b4[...]
    slot[2 * LANES : 3 * LANES, :] = c0[...]
    slot[3 * LANES :, :] = c1[...]
    table[0] = back("z", 5)
    table[1] = back("z", 4)
    table[2] = 8 + 2 * back("x", 2)
    table[3] = 9 + 2 * back("x", 2)
    block_logits(slot, panel, logits, part, table, slot.shape[0])


def first_col_kernel(logits, parts, mult, shifted, part, pot):
    pot[...] = jnp.log(mult[...].astype(F32)) - log_sum(parts[...])

    def block(b, carry):
        top, total = carry
        row = pot[pl.ds(b, 1), :]
        new = top
        for g, at in groups(b):
            x = logits[at, :] + column(row, g)
            shifted[at, :] = x
            new = jnp.maximum(new, x)
        total = total * jnp.exp(top - new)
        for g, at in groups(b):
            total = total + jnp.exp(shifted[at, :] - new)
        return new, total

    start = (jnp.full((SUB, COLS), -jnp.inf, F32), jnp.zeros((SUB, COLS), F32))
    top, total = lax.fori_loop(0, RB, block, start)
    peak = jnp.max(top, axis=0, keepdims=True)
    total = jnp.sum(total * jnp.exp(top - peak), axis=0, keepdims=True)
    put_dense(part, peak + jnp.log(total))


def scale_kernel(shifted, parts, caps, scaled, part):
    lse = log_sum(parts[...])
    pot = long_row(jnp.log(caps[...].astype(F32)) - lse)

    def block(b, carry):
        acc = jnp.zeros((SUB, LANES), F32)
        for g, at in groups(b):
            x = jnp.exp(shifted[at, :] + pot)
            scaled[at, :] = x
            acc = place(acc, jnp.sum(fold(x), axis=1, keepdims=True), g)
        part[pl.ds(b, 1), :] = jnp.sum(acc, axis=0, keepdims=True)
        return carry

    lax.fori_loop(0, RB, block, 0)


def col_kernel(scaled, parts, mult, part, u):
    u[...] = mult[...].astype(F32) / jnp.sum(parts[:, :RB, :], axis=0)

    def block(b, total):
        row = u[pl.ds(b, 1), :]
        for g, at in groups(b):
            total = total + scaled[at, :] * column(row, g)
        return total

    total = lax.fori_loop(0, RB, block, jnp.zeros((SUB, COLS), F32))
    put_dense(part, jnp.sum(total, axis=0, keepdims=True))


def row_kernel(scaled, parts, caps, part):
    caps_float = caps[...].astype(F32)
    v = long_row(caps_float / jnp.sum(parts[...], axis=0))

    def block(b, carry):
        acc = jnp.zeros((SUB, LANES), F32)
        for g, at in groups(b):
            acc = place(acc, jnp.sum(fold(scaled[at, :] * v), axis=1, keepdims=True), g)
        part[pl.ds(b, 1), :] = jnp.sum(acc, axis=0, keepdims=True)
        return carry

    lax.fori_loop(0, RB, block, 0)
    part[RB:, :] = jnp.broadcast_to(jnp.sum(caps_float), (SUB, LANES))


def plan_kernel(scaled, u, col_parts, caps, parts, plan):
    step = pl.program_id(0)
    cap_total = jnp.sum(parts[:, RB:, :], axis=0)
    v = caps[...].astype(F32) / jnp.sum(col_parts[...], axis=0)
    v = long_row(v * (float(SLOTS * ASSETS) / cap_total))
    x = step // 2
    upper = lax.rem(step, 2)
    for i in range(4):
        z = upper * 4 + i
        first = u[pl.ds(z, 1), :]
        second = u[pl.ds(8 + 2 * x + upper, 1), :]
        for g in range(4):
            at = pl.ds(pl.multiple_of((z * 4 + x) * 32 + SUB * g, SUB), SUB)
            to = 64 * i + SUB * g
            plan[to : to + SUB, :] = scaled[at, :] * column(first, 4 * x + g) * v
            at = pl.ds(pl.multiple_of(1024 + (x * 8 + z) * 32 + SUB * g, SUB), SUB)
            to = 64 * i + 32 + SUB * g
            plan[to : to + SUB, :] = scaled[at, :] * column(second, 4 * i + g) * v


def call(kernel, out_shape, scratch=(), **kwargs):
    return pl.pallas_call(
        kernel,
        out_shape=out_shape,
        scratch_shapes=list(scratch),
        compiler_params=pltpu.CompilerParams(vmem_limit_bytes=VMEM_LIMIT),
        **kwargs,
    )


def in_vmem(value):
    return pltpu.with_memory_space_constraint(value, pltpu.VMEM)


VM = pl.BlockSpec(memory_space=pltpu.VMEM)


def small(rows):
    return jax.ShapeDtypeStruct((rows, LANES), F32)


def per_device(slot_emb, asset_panel, mult, caps):
    mult = mult.reshape(4, 8, 2, 32)
    mult = jnp.concatenate(
        [mult[:, :, 0].transpose(1, 0, 2).reshape(8, LANES), mult[:, :, 1].reshape(8, LANES)]
    )
    caps = caps.reshape(CB, LANES)

    panels, panel_names = [], []
    for steps in (0, 1, 3, 2):
        piece = asset_panel if steps == 0 else shift(asset_panel, "y", steps)
        panels += [piece, shift(piece, "c", 1)]
        panel_names += [(steps, 0), (steps, 1)]

    first = [slot_emb[:32]]
    first += [shift(first[0], "x", steps) for steps in (1, 2, 3)]
    x = lax.axis_index("x")
    first = jnp.concatenate([lax.select_n(lax.rem(x - p + 4, 4), *first) for p in range(4)])
    first = ring_gather(first, "z")
    second = jnp.broadcast_to(slot_emb[None, 32:], (8, 32, EMB))
    second = lax.all_to_all(second, "z", 0, 0, tiled=True).reshape(256, EMB)
    second = ring_gather(second, "x")

    first[3][0], mult, caps = lax.optimization_barrier((first[3][0], mult, caps))

    block = pltpu.VMEM((ROWS, COLS), F32)
    panel_space = pltpu.VMEM((EMB, COLS), jnp.bfloat16)
    early = [first[k][0] for k in (0, 1, 7, 2, 6, 3)] + [second[j][0] for j in (0, 1, 3)]
    early_names = [("z", k, 0) for k in (0, 1, 7, 2, 6, 3)] + [("x", j, 0) for j in (0, 1, 3)]
    logits, part, panel = call(
        functools.partial(early_kernel, panel_names, early_names),
        (block, small(RB), panel_space),
        in_specs=[VM] * (len(panels) + len(early)),
        out_specs=(VM, VM, VM),
        scratch=[pltpu.VMEM((1536, EMB), jnp.bfloat16), pltpu.SMEM((12,), jnp.int32)],
        cost_estimate=pl.CostEstimate(flops=2 * 1536 * EMB * COLS, bytes_accessed=4 << 20, transcendentals=1536 * COLS),
    )(*panels, *early)
    late = [first[5][0], *first[4], *second[2]]
    logits, part = call(
        late_kernel,
        (block, small(RB)),
        in_specs=[VM] * (3 + len(late)),
        out_specs=(VM, VM),
        scratch=[pltpu.VMEM((512, EMB), jnp.bfloat16), pltpu.SMEM((4,), jnp.int32)],
        input_output_aliases={0: 0, 1: 1},
    )(in_vmem(logits), part, in_vmem(panel), *late)

    shifted, part = call(
        first_col_kernel, (block, small(CB)), in_specs=[VM] * 3, out_specs=(VM, VM),
        scratch=[pltpu.VMEM((RB, LANES), F32)],
    )(in_vmem(logits), over_asset(part), mult)
    parts = over_slot(part)

    scaled, part = call(scale_kernel, (block, small(RB)), in_specs=[VM] * 3, out_specs=(VM, VM))(
        in_vmem(shifted), parts, caps
    )
    for iteration in range(1, ITERS):
        row_parts = over_asset(part)
        part, u = call(col_kernel, (small(CB), small(RB)), in_specs=[VM] * 3, out_specs=(VM, VM))(
            in_vmem(scaled), row_parts, mult
        )
        parts = over_slot(part)
        if iteration < ITERS - 1:
            part = call(row_kernel, small(RB + SUB), in_specs=[VM] * 3, out_specs=VM)(in_vmem(scaled), parts, caps)
    return call(
        plan_kernel,
        jax.ShapeDtypeStruct((ROWS, COLS), F32),
        grid=(ROWS // 256,),
        in_specs=[VM] * 5,
        out_specs=pl.BlockSpec((256, COLS), lambda i: (i, 0)),
    )(in_vmem(scaled), u, parts, caps, row_parts)


def solution(mesh):
    fine = Mesh(mesh.devices.reshape(4, 2, 4, 8), ("y", "c", "x", "z"))
    slot, asset = ("y", "c"), ("x", "z")
    return jax.shard_map(
        per_device,
        mesh=fine,
        in_specs=(P(slot + asset, None), P(slot, asset), P(slot), P(asset)),
        out_specs=P(slot, asset),
        check_vma=False,
    )
```

```python
import functools

import jax
import jax.numpy as jnp
from jax import lax
from jax.experimental import pallas as pl
from jax.experimental.pallas import tpu as pltpu
from jax.sharding import Mesh, PartitionSpec as P

EMB = 768
ITERS = 3
SLOTS = 16384
ASSETS = 32768
ROWS, COLS = 2048, 1024
LANES, SUB = 128, 8
RB, CB = ROWS // LANES, COLS // LANES
VMEM_LIMIT = 28 << 20
BLOCK = 512
F32 = jnp.float32


def shift(value, axis, step):
    size = lax.axis_size(axis)
    return lax.ppermute(value, axis, [(i, (i + step) % size) for i in range(size)])


def ring_gather(value, axis):
    size = lax.axis_size(axis)
    shards = {0: [value]}
    ahead = behind = value
    for step in range(1, size // 2):
        ahead = shift(ahead, axis, 1)
        behind = shift(behind, axis, -1)
        shards[step] = [ahead]
        shards[size - step] = [behind]
    half = value.shape[0] // 2
    shards[size // 2] = [shift(ahead[:half], axis, 1), shift(behind[half:], axis, -1)]
    return shards


def over_asset(part):
    copies = jnp.broadcast_to(part[None], (32,) + part.shape)
    return lax.all_to_all(copies, ("x", "z"), 0, 0, tiled=True)


def over_slot(part):
    copies = jnp.broadcast_to(part[None], (8,) + part.shape)
    return lax.all_to_all(copies, ("y", "c"), 0, 0, tiled=True)


def iotas():
    lane = lax.broadcasted_iota(jnp.int32, (SUB, LANES), 1)
    row = lax.broadcasted_iota(jnp.int32, (SUB, LANES), 0)
    return lane, row


def column(row, g):
    lane, sub = iotas()
    return jnp.sum(jnp.where(lane == sub + SUB * g, row, 0.0), axis=1, keepdims=True)


def place(acc, col, g):
    lane, sub = iotas()
    return jnp.where(lane == sub + SUB * g, col, acc)


def long_row(dense):
    row = jnp.concatenate([dense[k : k + 1, :] for k in range(CB)], axis=1)
    return jnp.broadcast_to(row, (SUB, COLS))


def put_dense(ref, row):
    for k in range(CB):
        ref[k : k + 1, :] = row[:, LANES * k : LANES * (k + 1)]


def fold(wide):
    total = wide[:, :LANES]
    for k in range(1, CB):
        total = total + wide[:, LANES * k : LANES * (k + 1)]
    return total


def log_sum(parts):
    peak = jnp.max(parts, axis=0)
    return peak + jnp.log(jnp.sum(jnp.exp(parts - peak[None]), axis=0))


def groups(b):
    for g in range(LANES // SUB):
        yield g, pl.ds(pl.multiple_of(b * LANES + SUB * g, SUB), SUB)


def row_stats(logits, part, unit):
    peaks = []
    for g, at in groups(unit):
        x = logits[at, :]
        wide = x[:, :LANES]
        for k in range(1, CB):
            wide = jnp.maximum(wide, x[:, LANES * k : LANES * (k + 1)])
        peaks.append(jnp.max(wide, axis=1, keepdims=True))
    totals = []
    for g, at in groups(unit):
        totals.append(jnp.sum(fold(jnp.exp(logits[at, :] - peaks[g])), axis=1, keepdims=True))
    peak_row = jnp.zeros((SUB, LANES), F32)
    total_row = jnp.zeros((SUB, LANES), F32)
    for g in range(LANES // SUB):
        peak_row = place(peak_row, peaks[g], g)
        total_row = place(total_row, totals[g], g)
    peak_row = jnp.sum(peak_row, axis=0, keepdims=True)
    part[pl.ds(unit, 1), :] = peak_row + jnp.log(jnp.sum(total_row, axis=0, keepdims=True))


def block_logits(slot, panel, logits, part, table, count):
    def block(b, carry):
        rows = pl.ds(pl.multiple_of(b * BLOCK, BLOCK), BLOCK)
        value = jnp.dot(slot[rows, :], panel[...], preferred_element_type=F32) * EMB ** (-0.5)
        units = BLOCK // LANES
        for t in range(units):
            at = pl.ds(pl.multiple_of(table[b * units + t] * LANES, LANES), LANES)
            logits[at, :] = value[LANES * t : LANES * (t + 1), :]

        def stats(t, carry):
            row_stats(logits, part, table[b * units + t])
            return carry

        return lax.fori_loop(0, units, stats, carry)

    lax.fori_loop(0, count // BLOCK, block, 0)


def back(axis, steps):
    size = lax.axis_size(axis)
    return lax.rem(lax.axis_index(axis) - steps + size, size)


def put_slots(pieces, names, slot, table):
    at = 0
    for ref, (axis, steps, offset) in zip(pieces, names):
        rows = ref.shape[0]
        slot[at : at + rows, :] = ref[...]
        first = back("z", steps) if axis == "z" else 8 + 2 * back("x", steps) + offset
        for i in range(max(1, rows // LANES)):
            table[at // LANES + i] = first + i
        at += rows


def reorder_mult(mult):
    value = mult.astype(F32)
    lane, _ = iotas()
    rolled = [value] + [pltpu.roll(value, 32 * k, axis=1) for k in (1, 2, 3)]

    def moved(row, block, to):
        return rolled[(to - block) % 4][row : row + 1, :]

    def merged(pieces):
        out = pieces[0]
        for k in (1, 2, 3):
            out = jnp.where(lane[:1] >= 32 * k, pieces[k], out)
        return out

    rows = [merged([moved(4 * x + z // 2, 2 * (z % 2), x) for x in range(4)]) for z in range(8)]
    for x in range(4):
        for top in range(2):
            rows.append(merged([moved(4 * x + 2 * top + i // 2, 2 * (i % 2) + 1, i) for i in range(4)]))
    return rows


def first_kernel(panel_names, slot_names, *refs):
    n, m = len(panel_names), len(slot_names)
    own, mult, panels, slots = refs[0], refs[1], refs[2 : 2 + n], refs[2 + n : 2 + n + m]
    logits, part, panel, weight, slot, table, raw, sems = refs[2 + n + m :]
    at = pl.ds(pl.multiple_of((back("y", 0) * 2 + back("c", 0)) * 96, 32), 96)
    copy = pltpu.make_async_copy(own, panel.at[at], sems.at[0])
    copy.start()
    small_copy = pltpu.make_async_copy(mult, raw, sems.at[1])
    small_copy.start()
    for ref, (y_steps, c_steps) in zip(panels, panel_names):
        start = (back("y", y_steps) * 2 + back("c", c_steps)) * 96
        panel[pl.ds(pl.multiple_of(start, 32), 96), :] = ref[...]
    put_slots(slots, slot_names, slot, table)
    small_copy.wait()
    for i, row in enumerate(reorder_mult(raw[...])):
        weight[i : i + 1, :] = row
    copy.wait()
    block_logits(slot, panel, logits, part, table, slot.shape[0])


def more_kernel(slot_names, before, part_before, panel, *refs):
    m = len(slot_names)
    slots, (logits, part, slot, table) = refs[:m], refs[m:]
    del before, part_before
    put_slots(slots, slot_names, slot, table)
    block_logits(slot, panel, logits, part, table, slot.shape[0])


def first_col_kernel(logits, parts, mult, shifted, part, pot):
    pot[...] = jnp.log(mult[...]) - log_sum(parts[...])

    def block(b, carry):
        top, total = carry
        row = pot[pl.ds(b, 1), :]
        new = top
        for g, at in groups(b):
            x = logits[at, :] + column(row, g)
            shifted[at, :] = x
            new = jnp.maximum(new, x)
        total = total * jnp.exp(top - new)
        for g, at in groups(b):
            total = total + jnp.exp(shifted[at, :] - new)
        return new, total

    start = (jnp.full((SUB, COLS), -jnp.inf, F32), jnp.zeros((SUB, COLS), F32))
    top, total = lax.fori_loop(0, RB, block, start)
    peak = jnp.max(top, axis=0, keepdims=True)
    total = jnp.sum(total * jnp.exp(top - peak), axis=0, keepdims=True)
    put_dense(part, peak + jnp.log(total))


def scale_kernel(shifted, parts, caps, scaled, part):
    lse = log_sum(parts[...])
    pot = long_row(jnp.log(caps[...].astype(F32)) - lse)

    def block(b, carry):
        acc = jnp.zeros((SUB, LANES), F32)
        for g, at in groups(b):
            x = jnp.exp(shifted[at, :] + pot)
            scaled[at, :] = x
            acc = place(acc, jnp.sum(fold(x), axis=1, keepdims=True), g)
        part[pl.ds(b, 1), :] = jnp.sum(acc, axis=0, keepdims=True)
        return carry

    lax.fori_loop(0, RB, block, 0)


def col_kernel(scaled, parts, mult, part, u):
    rows = jnp.sum(parts[...], axis=0)
    u[...] = mult[...] / rows
    if part.shape[0] > CB:
        part[CB:, :] = jnp.broadcast_to(jnp.sum(rows), (SUB, LANES))

    def block(b, total):
        row = u[pl.ds(b, 1), :]
        for g, at in groups(b):
            total = total + scaled[at, :] * column(row, g)
        return total

    total = lax.fori_loop(0, RB, block, jnp.zeros((SUB, COLS), F32))
    put_dense(part, jnp.sum(total, axis=0, keepdims=True))


def row_kernel(scaled, parts, caps, part):
    caps_float = caps[...].astype(F32)
    v = long_row(caps_float / jnp.sum(parts[:, :CB], axis=0))

    def block(b, carry):
        acc = jnp.zeros((SUB, LANES), F32)
        for g, at in groups(b):
            acc = place(acc, jnp.sum(fold(scaled[at, :] * v), axis=1, keepdims=True), g)
        part[pl.ds(b, 1), :] = jnp.sum(acc, axis=0, keepdims=True)
        return carry

    lax.fori_loop(0, RB, block, 0)


def plan_kernel(scaled, u, col_parts, caps, total_parts, plan):
    step = pl.program_id(0)
    cap_total = jnp.sum(total_parts[:, CB:], axis=0)
    v = caps[...].astype(F32) / jnp.sum(col_parts[...], axis=0)
    v = long_row(v * (float(SLOTS * ASSETS) / cap_total))
    x = step // 2
    upper = lax.rem(step, 2)
    for i in range(4):
        z = upper * 4 + i
        first = u[pl.ds(z, 1), :]
        second = u[pl.ds(8 + 2 * x + upper, 1), :]
        for g in range(4):
            at = pl.ds(pl.multiple_of((z * 4 + x) * 32 + SUB * g, SUB), SUB)
            to = 64 * i + SUB * g
            plan[to : to + SUB, :] = scaled[at, :] * column(first, 4 * x + g) * v
            at = pl.ds(pl.multiple_of(1024 + (x * 8 + z) * 32 + SUB * g, SUB), SUB)
            to = 64 * i + 32 + SUB * g
            plan[to : to + SUB, :] = scaled[at, :] * column(second, 4 * i + g) * v


def call(kernel, out_shape, scratch=(), **kwargs):
    return pl.pallas_call(
        kernel,
        out_shape=out_shape,
        scratch_shapes=list(scratch),
        compiler_params=pltpu.CompilerParams(vmem_limit_bytes=VMEM_LIMIT),
        **kwargs,
    )


def in_vmem(value):
    return pltpu.with_memory_space_constraint(value, pltpu.VMEM)


def in_hbm(value):
    return pltpu.with_memory_space_constraint(value, pltpu.HBM)


VM = pl.BlockSpec(memory_space=pltpu.VMEM)


def small(rows):
    return jax.ShapeDtypeStruct((rows, LANES), F32)


def per_device(slot_emb, asset_panel, mult, caps):
    mult = mult.reshape(RB, LANES)
    caps = caps.reshape(CB, LANES)

    panels, panel_names = [shift(asset_panel, "c", 1)], [(0, 1)]
    for steps in (1, 3, 2):
        piece = shift(asset_panel, "y", steps)
        panels += [piece, shift(piece, "c", 1)]
        panel_names += [(steps, 0), (steps, 1)]

    first = [slot_emb[:32]]
    first += [shift(first[0], "x", steps) for steps in (1, 2, 3)]
    x = lax.axis_index("x")
    first = jnp.concatenate([lax.select_n(lax.rem(x - p + 4, 4), *first) for p in range(4)])
    ahead, behind = [first], [first]
    for step in range(3):
        ahead.append(shift(ahead[-1], "z", 1))
        behind.append(shift(behind[-1], "z", -1))
    second = jnp.broadcast_to(slot_emb[None, 32:], (8, 32, EMB))
    second = lax.all_to_all(second, "z", 0, 0, tiled=True).reshape(256, EMB)
    second = ring_gather(second, "x")

    block = pltpu.VMEM((ROWS, COLS), F32)

    def take(pieces):
        names = [name for name, piece in pieces]
        pieces = [piece for name, piece in pieces]
        rows = sum(p.shape[0] for p in pieces)
        scratch = [pltpu.VMEM((rows, EMB), jnp.bfloat16), pltpu.SMEM((rows // LANES,), jnp.int32)]
        cost = pl.CostEstimate(flops=2 * rows * EMB * COLS, bytes_accessed=rows * 8192, transcendentals=rows * COLS)
        return names, pieces, scratch, cost

    def some(kind, k):
        if kind == "x":
            return [(("x", k, i), piece) for i, piece in enumerate(second[k])]
        if k == 4:
            return [(("z", 4, 0), shift(ahead[3][:64], "z", 1)), (("z", 4, 0), shift(behind[3][64:], "z", -1))]
        return [(("z", k, 0), ahead[k] if k < 4 else behind[8 - k])]

    names, pieces, scratch, cost = take(some("z", 0) + some("z", 1) + some("x", 0))
    hbm = pl.BlockSpec(memory_space=pltpu.HBM)
    logits, part, panel, weight = call(
        functools.partial(first_kernel, panel_names, names),
        (block, small(RB), pltpu.VMEM((EMB, COLS), jnp.bfloat16), small(RB)),
        in_specs=[hbm, hbm] + [VM] * (len(panels) + len(pieces)),
        out_specs=(VM,) * 4,
        scratch=scratch + [pltpu.VMEM((RB, LANES), jnp.int32), pltpu.SemaphoreType.DMA((2,))],
        cost_estimate=cost,
    )(in_hbm(asset_panel), in_hbm(mult), *panels, *pieces)
    ahead[3], behind[3], part = lax.optimization_barrier((ahead[3], behind[3], part))
    middle = some("z", 7) + some("z", 2) + some("z", 6) + some("z", 3) + some("x", 1) + some("x", 3)
    last = some("z", 5) + some("z", 4) + some("x", 2)
    for pieces in (middle, last):
        names, pieces, scratch, cost = take(pieces)
        logits, part = call(
            functools.partial(more_kernel, names),
            (block, small(RB)),
            in_specs=[VM] * (3 + len(pieces)),
            out_specs=(VM, VM),
            scratch=scratch,
            input_output_aliases={0: 0, 1: 1},
            cost_estimate=cost,
        )(in_vmem(logits), part, in_vmem(panel), *pieces)

    shifted, part = call(
        first_col_kernel, (block, small(CB)), in_specs=[VM] * 3, out_specs=(VM, VM),
        scratch=[pltpu.VMEM((RB, LANES), F32)],
    )(in_vmem(logits), over_asset(part), weight)
    parts = over_slot(part)

    scaled, part = call(scale_kernel, (block, small(RB)), in_specs=[VM] * 3, out_specs=(VM, VM))(
        in_vmem(shifted), parts, caps
    )
    for iteration in range(1, ITERS):
        rows = CB + SUB if iteration == 1 else CB
        part, u = call(col_kernel, (small(rows), small(RB)), in_specs=[VM] * 3, out_specs=(VM, VM))(
            in_vmem(scaled), over_asset(part), weight
        )
        parts = over_slot(part)
        if iteration == 1:
            total_parts = parts
        if iteration < ITERS - 1:
            part = call(row_kernel, small(RB), in_specs=[VM] * 3, out_specs=VM)(in_vmem(scaled), parts, caps)
    return call(
        plan_kernel,
        jax.ShapeDtypeStruct((ROWS, COLS), F32),
        grid=(ROWS // 256,),
        in_specs=[VM] * 5,
        out_specs=pl.BlockSpec((256, COLS), lambda i: (i, 0)),
    )(in_vmem(scaled), u, parts, caps, total_parts)


def solution(mesh):
    fine = Mesh(mesh.devices.reshape(4, 2, 4, 8), ("y", "c", "x", "z"))
    slot, asset = ("y", "c"), ("x", "z")
    return jax.shard_map(
        per_device,
        mesh=fine,
        in_specs=(P(slot + asset, None), P(slot, asset), P(slot), P(asset)),
        out_specs=P(slot, asset),
        check_vma=False,
    )
```

```python
import functools

import jax
import jax.numpy as jnp
from jax import lax
from jax.experimental import pallas as pl
from jax.experimental.pallas import tpu as pltpu
from jax.sharding import Mesh, PartitionSpec as P

EMB = 768
ITERS = 3
SLOTS = 16384
ASSETS = 32768
ROWS, COLS = 2048, 1024
LANES, SUB = 128, 8
RB, CB = ROWS // LANES, COLS // LANES
VMEM_LIMIT = 28 << 20
BLOCK = 512
F32 = jnp.float32


def shift(value, axis, step):
    size = lax.axis_size(axis)
    return lax.ppermute(value, axis, [(i, (i + step) % size) for i in range(size)])


def ring_gather(value, axis):
    size = lax.axis_size(axis)
    shards = {0: [value]}
    ahead = behind = value
    for step in range(1, size // 2):
        ahead = shift(ahead, axis, 1)
        behind = shift(behind, axis, -1)
        shards[step] = [ahead]
        shards[size - step] = [behind]
    half = value.shape[0] // 2
    shards[size // 2] = [shift(ahead[:half], axis, 1), shift(behind[half:], axis, -1)]
    return shards


def over_asset(part):
    copies = jnp.broadcast_to(part[None], (32,) + part.shape)
    return lax.all_to_all(copies, ("x", "z"), 0, 0, tiled=True)


def over_slot(part):
    copies = jnp.broadcast_to(part[None], (8,) + part.shape)
    return lax.all_to_all(copies, ("y", "c"), 0, 0, tiled=True)


def iotas():
    lane = lax.broadcasted_iota(jnp.int32, (SUB, LANES), 1)
    row = lax.broadcasted_iota(jnp.int32, (SUB, LANES), 0)
    return lane, row


def column(row, g):
    lane, sub = iotas()
    return jnp.sum(jnp.where(lane == sub + SUB * g, row, 0.0), axis=1, keepdims=True)


def place(acc, col, g):
    lane, sub = iotas()
    return jnp.where(lane == sub + SUB * g, col, acc)


def long_row(dense):
    row = jnp.concatenate([dense[k : k + 1, :] for k in range(CB)], axis=1)
    return jnp.broadcast_to(row, (SUB, COLS))


def put_dense(ref, row):
    for k in range(CB):
        ref[k : k + 1, :] = row[:, LANES * k : LANES * (k + 1)]


def fold(wide):
    total = wide[:, :LANES]
    for k in range(1, CB):
        total = total + wide[:, LANES * k : LANES * (k + 1)]
    return total


def log_sum(parts):
    peak = jnp.max(parts, axis=0)
    return peak + jnp.log(jnp.sum(jnp.exp(parts - peak[None]), axis=0))


def groups(b):
    for g in range(LANES // SUB):
        yield g, pl.ds(pl.multiple_of(b * LANES + SUB * g, SUB), SUB)


def row_stats(logits, gauss, peak, part, unit):
    peaks = []
    for g, at in groups(unit):
        x = logits[at, :]
        wide = x[:, :LANES]
        for k in range(1, CB):
            wide = jnp.maximum(wide, x[:, LANES * k : LANES * (k + 1)])
        peaks.append(jnp.max(wide, axis=1, keepdims=True))
    peak_row = jnp.zeros((SUB, LANES), F32)
    total_row = jnp.zeros((SUB, LANES), F32)
    for g, at in groups(unit):
        x = jnp.exp(logits[at, :] - peaks[g])
        gauss[at, :] = x
        total_row = place(total_row, jnp.sum(fold(x), axis=1, keepdims=True), g)
        peak_row = place(peak_row, peaks[g], g)
    peak_row = jnp.sum(peak_row, axis=0, keepdims=True)
    peak[pl.ds(unit, 1), :] = peak_row
    part[pl.ds(unit, 1), :] = peak_row + jnp.log(jnp.sum(total_row, axis=0, keepdims=True))


def block_logits(slot, panel, outs, table, count):
    logits = outs[0]
    units = BLOCK // LANES

    def block(b, carry):
        rows = pl.ds(pl.multiple_of(b * BLOCK, BLOCK), BLOCK)
        value = jnp.dot(slot[rows, :], panel[...], preferred_element_type=F32) * EMB ** (-0.5)
        for t in range(units):
            at = pl.ds(pl.multiple_of(table[b * units + t] * LANES, LANES), LANES)
            logits[at, :] = value[LANES * t : LANES * (t + 1), :]

        def stats(t, carry):
            row_stats(*outs, table[b * units + t])
            return carry

        return lax.fori_loop(0, units, stats, carry)

    lax.fori_loop(0, count // BLOCK, block, 0)


def back(axis, steps):
    size = lax.axis_size(axis)
    return lax.rem(lax.axis_index(axis) - steps + size, size)


def put_slots(pieces, names, slot, table):
    at = 0
    for ref, (axis, steps, offset) in zip(pieces, names):
        rows = ref.shape[0]
        unit = at // LANES
        if axis == "z":
            table[unit] = back("z", steps)
            for j in range(rows // 32):
                to = pl.multiple_of(unit * LANES + back("x", offset + j) * 32, 32)
                slot[pl.ds(to, 32), :] = ref[32 * j : 32 * (j + 1), :]
        else:
            slot[at : at + rows, :] = ref[...]
            for i in range(rows // LANES):
                table[unit + i] = 8 + 2 * back("x", steps) + offset + i
        at += rows


def reorder_mult(mult):
    value = mult.astype(F32)
    lane, _ = iotas()
    rolled = [value] + [pltpu.roll(value, 32 * k, axis=1) for k in (1, 2, 3)]

    def moved(row, block, to):
        return rolled[(to - block) % 4][row : row + 1, :]

    def merged(pieces):
        out = pieces[0]
        for k in (1, 2, 3):
            out = jnp.where(lane[:1] >= 32 * k, pieces[k], out)
        return out

    rows = [merged([moved(4 * x + z // 2, 2 * (z % 2), x) for x in range(4)]) for z in range(8)]
    for x in range(4):
        for top in range(2):
            rows.append(merged([moved(4 * x + 2 * top + i // 2, 2 * (i % 2) + 1, i) for i in range(4)]))
    return rows


def first_kernel(panel_names, slot_names, *refs):
    n, m = len(panel_names), len(slot_names)
    own, mult, panels, slots = refs[0], refs[1], refs[2 : 2 + n], refs[2 + n : 2 + n + m]
    *outs, panel, weight, slot, table, raw, sems = refs[2 + n + m :]
    at = pl.ds(pl.multiple_of((back("y", 0) * 2 + back("c", 0)) * 96, 32), 96)
    copy = pltpu.make_async_copy(own, panel.at[at], sems.at[0])
    copy.start()
    small_copy = pltpu.make_async_copy(mult, raw, sems.at[1])
    small_copy.start()
    for ref, (y_steps, c_steps) in zip(panels, panel_names):
        start = (back("y", y_steps) * 2 + back("c", c_steps)) * 96
        panel[pl.ds(pl.multiple_of(start, 32), 96), :] = ref[...]
    put_slots(slots, slot_names, slot, table)
    small_copy.wait()
    for i, row in enumerate(reorder_mult(raw[...])):
        weight[i : i + 1, :] = row
    copy.wait()
    block_logits(slot, panel, outs, table, slot.shape[0])


def more_kernel(slot_names, logits, gauss, peak, part, panel, *refs):
    m = len(slot_names)
    del logits, gauss, peak, part
    slots, (*outs, slot, table) = refs[:m], refs[m:]
    put_slots(slots, slot_names, slot, table)
    block_logits(slot, panel, outs, table, slot.shape[0])


def weighted_cols(gauss, weights):
    def block(b, total):
        row = weights[pl.ds(b, 1), :]
        for g, at in groups(b):
            total = total + gauss[at, :] * column(row, g)
        return total

    total = lax.fori_loop(0, RB, block, jnp.zeros((SUB, COLS), F32))
    return jnp.sum(total, axis=0, keepdims=True)


def weighted_rows(gauss, weights, part):
    def block(b, carry):
        acc = jnp.zeros((SUB, LANES), F32)
        for g, at in groups(b):
            acc = place(acc, jnp.sum(fold(gauss[at, :] * weights), axis=1, keepdims=True), g)
        part[pl.ds(b, 1), :] = jnp.sum(acc, axis=0, keepdims=True)
        return carry

    lax.fori_loop(0, RB, block, 0)


def first_col_kernel(logits, before, parts, weight, peak, gauss, row_scale, col_shift, part, pot):
    del before
    pot[...] = jnp.log(weight[...]) - log_sum(parts[...])
    row_scale[...] = jnp.exp(peak[...] + pot[...])
    total = weighted_cols(gauss, row_scale)
    col_shift[...] = jnp.zeros((CB, LANES), F32)
    put_dense(part, jnp.log(total))

    @pl.when(jnp.min(total) < 1e-20)
    def _():
        def shift_block(b, top):
            row = pot[pl.ds(b, 1), :]
            for g, at in groups(b):
                x = logits[at, :] + column(row, g)
                gauss[at, :] = x
                top = jnp.maximum(top, x)
            return top

        top = lax.fori_loop(0, RB, shift_block, jnp.full((SUB, COLS), -jnp.inf, F32))
        top = jnp.max(top, axis=0, keepdims=True)
        wide = jnp.broadcast_to(top, (SUB, COLS))

        def exp_block(b, total):
            for g, at in groups(b):
                x = jnp.exp(gauss[at, :] - wide)
                gauss[at, :] = x
                total = total + x
            return total

        total = lax.fori_loop(0, RB, exp_block, jnp.zeros((SUB, COLS), F32))
        row_scale[...] = jnp.ones((RB, LANES), F32)
        put_dense(col_shift, top)
        put_dense(part, top + jnp.log(jnp.sum(total, axis=0, keepdims=True)))


def first_row_kernel(gauss, parts, caps, row_scale, col_shift, part, col_scale):
    pot = jnp.log(caps[...].astype(F32)) - log_sum(parts[...])
    col_scale[...] = jnp.exp(col_shift[...] + pot)
    weighted_rows(gauss, long_row(col_scale[...]), part)
    part[...] = part[...] * row_scale[...]


def row_kernel(gauss, parts, caps, row_scale, col_scale, part):
    v = caps[...].astype(F32) / jnp.sum(parts[:, :CB], axis=0)
    weighted_rows(gauss, long_row(v * col_scale[...]), part)
    part[...] = part[...] * row_scale[...]


def col_kernel(gauss, parts, weight, row_scale, col_scale, part, u):
    rows = jnp.sum(parts[...], axis=0)
    u[...] = weight[...] / rows * row_scale[...]
    put_dense(part, weighted_cols(gauss, u))
    part[:CB, :] = part[:CB, :] * col_scale[...]
    part[CB:, :] = jnp.broadcast_to(jnp.sum(rows), (SUB, LANES))


def last_col_kernel(gauss, parts, weight, row_scale, col_scale, scaled, part, u):
    u[...] = weight[...] / jnp.sum(parts[...], axis=0) * row_scale[...]

    def block(half):
        def body(b, total):
            row = u[pl.ds(8 * half + b, 1), :]
            for g, at in groups(8 * half + b):
                i, r = g // 4, g % 4
                a = 8 * i + b if half == 0 else 4 * b + i
                value = gauss[at, :] * column(row, g)
                scaled[pl.ds(pl.multiple_of(a * 64 + 32 * half + SUB * r, SUB), SUB), :] = value
                total = total + value
            return total

        return body

    total = lax.fori_loop(0, 8, block(0), jnp.zeros((SUB, COLS), F32))
    total = lax.fori_loop(0, 8, block(1), total)
    put_dense(part, jnp.sum(total, axis=0, keepdims=True))
    part[...] = part[...] * col_scale[...]


def plan_kernel(scaled, parts, total_parts, caps, col_scale, plan, v):
    step = pl.program_id(0)

    @pl.when(step == 0)
    def _():
        cap_total = jnp.sum(total_parts[:, CB:], axis=0)
        factor = float(SLOTS * ASSETS) / cap_total
        v[...] = long_row(caps[...].astype(F32) / jnp.sum(parts[...], axis=0) * col_scale[...] * factor)

    rows = plan.shape[0]
    for g in range(rows // SUB):
        at = pl.ds(pl.multiple_of(step * rows + SUB * g, SUB), SUB)
        plan[SUB * g : SUB * (g + 1), :] = scaled[at, :] * v[...]


def call(kernel, out_shape, scratch=(), **kwargs):
    return pl.pallas_call(
        kernel,
        out_shape=out_shape,
        scratch_shapes=list(scratch),
        compiler_params=pltpu.CompilerParams(vmem_limit_bytes=VMEM_LIMIT),
        **kwargs,
    )


def in_vmem(value):
    return pltpu.with_memory_space_constraint(value, pltpu.VMEM)


def in_hbm(value):
    return pltpu.with_memory_space_constraint(value, pltpu.HBM)


VM = pl.BlockSpec(memory_space=pltpu.VMEM)


def small(rows):
    return jax.ShapeDtypeStruct((rows, LANES), F32)


def per_device(slot_emb, asset_panel, mult, caps):
    mult = mult.reshape(RB, LANES)
    caps = caps.reshape(CB, LANES)

    panels, panel_names = [shift(asset_panel, "c", 1)], [(0, 1)]
    for steps in (1, 3, 2):
        piece = shift(asset_panel, "y", steps)
        panels += [piece, shift(piece, "c", 1)]
        panel_names += [(steps, 0), (steps, 1)]

    first = [slot_emb[:32]]
    first += [shift(first[0], "x", steps) for steps in (1, 2, 3)]
    first = jnp.concatenate(first)
    ahead, behind = [first], [first]
    for step in range(3):
        ahead.append(shift(ahead[-1], "z", 1))
        behind.append(shift(behind[-1], "z", -1))
    second = jnp.broadcast_to(slot_emb[None, 32:], (8, 32, EMB))
    second = lax.all_to_all(second, "z", 0, 0, tiled=True).reshape(256, EMB)
    second = ring_gather(second, "x")

    block = pltpu.VMEM((ROWS, COLS), F32)

    def take(pieces):
        names = [name for name, piece in pieces]
        pieces = [piece for name, piece in pieces]
        rows = sum(p.shape[0] for p in pieces)
        scratch = [pltpu.VMEM((rows, EMB), jnp.bfloat16), pltpu.SMEM((rows // LANES,), jnp.int32)]
        cost = pl.CostEstimate(flops=2 * rows * EMB * COLS, bytes_accessed=rows * 8192, transcendentals=rows * COLS)
        return names, pieces, scratch, cost

    def some(kind, k):
        if kind == "x":
            return [(("x", k, i), piece) for i, piece in enumerate(second[k])]
        if k == 4:
            return [(("z", 4, 0), shift(ahead[3][:64], "z", 1)), (("z", 4, 2), shift(behind[3][64:], "z", -1))]
        return [(("z", k, 0), ahead[k] if k < 4 else behind[8 - k])]

    names, pieces, scratch, cost = take(some("z", 0) + some("z", 1) + some("x", 0))
    hbm = pl.BlockSpec(memory_space=pltpu.HBM)
    logits, gauss, peak, part, panel, weight = call(
        functools.partial(first_kernel, panel_names, names),
        (block, block, small(RB), small(RB), pltpu.VMEM((EMB, COLS), jnp.bfloat16), small(RB)),
        in_specs=[hbm, hbm] + [VM] * (len(panels) + len(pieces)),
        out_specs=(VM,) * 6,
        scratch=scratch + [pltpu.VMEM((RB, LANES), jnp.int32), pltpu.SemaphoreType.DMA((2,))],
        cost_estimate=cost,
    )(in_hbm(asset_panel), in_hbm(mult), *panels, *pieces)
    ahead[3], behind[3], part = lax.optimization_barrier((ahead[3], behind[3], part))
    middle = some("z", 7) + some("z", 2) + some("z", 6) + some("z", 3) + some("x", 1) + some("x", 3)
    last = some("z", 5) + some("z", 4) + some("x", 2)
    for pieces in (middle, last):
        names, pieces, scratch, cost = take(pieces)
        logits, gauss, peak, part = call(
            functools.partial(more_kernel, names),
            (block, block, small(RB), small(RB)),
            in_specs=[VM] * (5 + len(pieces)),
            out_specs=(VM,) * 4,
            scratch=scratch,
            input_output_aliases={0: 0, 1: 1, 2: 2, 3: 3},
            cost_estimate=cost,
        )(in_vmem(logits), in_vmem(gauss), peak, part, in_vmem(panel), *pieces)

    gauss, row_scale, col_shift, part = call(
        first_col_kernel,
        (block, small(RB), small(CB), small(CB)),
        in_specs=[VM] * 5,
        out_specs=(VM,) * 4,
        scratch=[pltpu.VMEM((RB, LANES), F32)],
        input_output_aliases={1: 0},
    )(in_vmem(logits), in_vmem(gauss), over_asset(part), weight, peak)
    part, col_scale = call(first_row_kernel, (small(RB), small(CB)), in_specs=[VM] * 5, out_specs=(VM, VM))(
        in_vmem(gauss), over_slot(part), caps, row_scale, col_shift
    )
    u_space = [pltpu.VMEM((RB, LANES), F32)]
    for iteration in range(1, ITERS - 1):
        part = call(col_kernel, small(CB + SUB), in_specs=[VM] * 5, out_specs=VM, scratch=u_space)(
            in_vmem(gauss), over_asset(part), weight, row_scale, col_scale
        )
        total_parts = over_slot(part)
        part = call(row_kernel, small(RB), in_specs=[VM] * 5, out_specs=VM)(
            in_vmem(gauss), total_parts, caps, row_scale, col_scale
        )
    scaled, part = call(last_col_kernel, (block, small(CB)), in_specs=[VM] * 5, out_specs=(VM, VM), scratch=u_space)(
        in_vmem(gauss), over_asset(part), weight, row_scale, col_scale
    )
    return call(
        plan_kernel,
        jax.ShapeDtypeStruct((ROWS, COLS), F32),
        grid=(ROWS // 256,),
        in_specs=[VM] * 5,
        out_specs=pl.BlockSpec((256, COLS), lambda i: (i, 0)),
        scratch=[pltpu.VMEM((SUB, COLS), F32)],
    )(in_vmem(scaled), over_slot(part), total_parts, caps, col_scale)


def solution(mesh):
    fine = Mesh(mesh.devices.reshape(4, 2, 4, 8), ("y", "c", "x", "z"))
    slot, asset = ("y", "c"), ("x", "z")
    return jax.shard_map(
        per_device,
        mesh=fine,
        in_specs=(P(slot + asset, None), P(slot, asset), P(slot), P(asset)),
        out_specs=P(slot, asset),
        check_vma=False,
    )
```

```python
import functools

import jax
import jax.numpy as jnp
from jax import lax
from jax.experimental import pallas as pl
from jax.experimental.pallas import tpu as pltpu
from jax.sharding import Mesh, PartitionSpec as P

EMB = 768
ITERS = 3
SLOTS = 16384
ASSETS = 32768
ROWS, COLS = 2048, 1024
LANES, SUB = 128, 8
RB, CB = ROWS // LANES, COLS // LANES
VMEM_LIMIT = 28 << 20
BLOCK = 512
F32 = jnp.float32


def shift(value, axis, step):
    size = lax.axis_size(axis)
    return lax.ppermute(value, axis, [(i, (i + step) % size) for i in range(size)])


def ring_gather(value, axis):
    size = lax.axis_size(axis)
    shards = {0: [value]}
    ahead = behind = value
    for step in range(1, size // 2):
        ahead = shift(ahead, axis, 1)
        behind = shift(behind, axis, -1)
        shards[step] = [ahead]
        shards[size - step] = [behind]
    half = value.shape[0] // 2
    shards[size // 2] = [shift(ahead[:half], axis, 1), shift(behind[half:], axis, -1)]
    return shards


def over_asset(part):
    copies = jnp.broadcast_to(part[None], (32,) + part.shape)
    return lax.all_to_all(copies, ("x", "z"), 0, 0, tiled=True)


def over_slot(part):
    copies = jnp.broadcast_to(part[None], (8,) + part.shape)
    return lax.all_to_all(copies, ("y", "c"), 0, 0, tiled=True)


def iotas():
    lane = lax.broadcasted_iota(jnp.int32, (SUB, LANES), 1)
    row = lax.broadcasted_iota(jnp.int32, (SUB, LANES), 0)
    return lane, row


def column(row, g):
    lane, sub = iotas()
    return jnp.sum(jnp.where(lane == sub + SUB * g, row, 0.0), axis=1, keepdims=True)


def place(acc, col, g):
    lane, sub = iotas()
    return jnp.where(lane == sub + SUB * g, col, acc)


def long_row(dense):
    row = jnp.concatenate([dense[k : k + 1, :] for k in range(CB)], axis=1)
    return jnp.broadcast_to(row, (SUB, COLS))


def put_dense(ref, row):
    for k in range(CB):
        ref[k : k + 1, :] = row[:, LANES * k : LANES * (k + 1)]


def fold(wide):
    total = wide[:, :LANES]
    for k in range(1, CB):
        total = total + wide[:, LANES * k : LANES * (k + 1)]
    return total


def log_sum(parts):
    peak = jnp.max(parts, axis=0)
    return peak + jnp.log(jnp.sum(jnp.exp(parts - peak[None]), axis=0))


def groups(b):
    for g in range(LANES // SUB):
        yield g, pl.ds(pl.multiple_of(b * LANES + SUB * g, SUB), SUB)


def row_stats(logits, gauss, peak, part, unit):
    peaks = []
    for g, at in groups(unit):
        x = logits[at, :]
        wide = x[:, :LANES]
        for k in range(1, CB):
            wide = jnp.maximum(wide, x[:, LANES * k : LANES * (k + 1)])
        peaks.append(jnp.max(wide, axis=1, keepdims=True))
    peak_row = jnp.zeros((SUB, LANES), F32)
    total_row = jnp.zeros((SUB, LANES), F32)
    for g, at in groups(unit):
        x = jnp.exp(logits[at, :] - peaks[g])
        gauss[at, :] = x
        total_row = place(total_row, jnp.sum(fold(x), axis=1, keepdims=True), g)
        peak_row = place(peak_row, peaks[g], g)
    peak_row = jnp.sum(peak_row, axis=0, keepdims=True)
    peak[pl.ds(unit, 1), :] = peak_row
    part[pl.ds(unit, 1), :] = peak_row + jnp.log(jnp.sum(total_row, axis=0, keepdims=True))


def block_logits(slot, panel, outs, table, count):
    logits = outs[0]
    units = BLOCK // LANES

    def block(b, carry):
        rows = pl.ds(pl.multiple_of(b * BLOCK, BLOCK), BLOCK)
        value = jnp.dot(slot[rows, :], panel[...], preferred_element_type=F32) * EMB ** (-0.5)
        for t in range(units):
            at = pl.ds(pl.multiple_of(table[b * units + t] * LANES, LANES), LANES)
            logits[at, :] = value[LANES * t : LANES * (t + 1), :]

        def stats(t, carry):
            row_stats(*outs, table[b * units + t])
            return carry

        return lax.fori_loop(0, units, stats, carry)

    lax.fori_loop(0, count // BLOCK, block, 0)


def back(axis, steps):
    size = lax.axis_size(axis)
    return lax.rem(lax.axis_index(axis) - steps + size, size)


def put_slots(pieces, names, slot, table):
    at = 0
    for ref, (axis, steps, offset) in zip(pieces, names):
        rows = ref.shape[0]
        unit = at // LANES
        if axis == "z":
            table[unit] = back("z", steps)
            for j in range(rows // 32):
                to = pl.multiple_of(unit * LANES + back("x", offset + j) * 32, 32)
                slot[pl.ds(to, 32), :] = ref[32 * j : 32 * (j + 1), :]
        else:
            slot[at : at + rows, :] = ref[...]
            for i in range(rows // LANES):
                table[unit + i] = 8 + 2 * back("x", steps) + offset + i
        at += rows


def reorder_mult(mult):
    value = mult.astype(F32)
    lane, _ = iotas()
    rolled = [value] + [pltpu.roll(value, 32 * k, axis=1) for k in (1, 2, 3)]

    def moved(row, block, to):
        return rolled[(to - block) % 4][row : row + 1, :]

    def merged(pieces):
        out = pieces[0]
        for k in (1, 2, 3):
            out = jnp.where(lane[:1] >= 32 * k, pieces[k], out)
        return out

    rows = [merged([moved(4 * x + z // 2, 2 * (z % 2), x) for x in range(4)]) for z in range(8)]
    for x in range(4):
        for top in range(2):
            rows.append(merged([moved(4 * x + 2 * top + i // 2, 2 * (i % 2) + 1, i) for i in range(4)]))
    return rows


def first_kernel(panel_names, slot_names, *refs):
    n, m = len(panel_names), len(slot_names)
    own, mult, panels, slots = refs[0], refs[1], refs[2 : 2 + n], refs[2 + n : 2 + n + m]
    *outs, panel, weight, slot, table, raw, sems = refs[2 + n + m :]
    at = pl.ds(pl.multiple_of((back("y", 0) * 2 + back("c", 0)) * 96, 32), 96)
    copy = pltpu.make_async_copy(own, panel.at[at], sems.at[0])
    copy.start()
    small_copy = pltpu.make_async_copy(mult, raw, sems.at[1])
    small_copy.start()
    for ref, (y_steps, c_steps) in zip(panels, panel_names):
        start = (back("y", y_steps) * 2 + back("c", c_steps)) * 96
        panel[pl.ds(pl.multiple_of(start, 32), 96), :] = ref[...]
    put_slots(slots, slot_names, slot, table)
    small_copy.wait()
    for i, row in enumerate(reorder_mult(raw[...])):
        weight[i : i + 1, :] = row
    copy.wait()
    block_logits(slot, panel, outs, table, slot.shape[0])


def more_kernel(slot_names, logits, gauss, peak, part, panel, *refs):
    m = len(slot_names)
    del logits, gauss, peak, part
    slots, (*outs, slot, table) = refs[:m], refs[m:]
    put_slots(slots, slot_names, slot, table)
    block_logits(slot, panel, outs, table, slot.shape[0])


def weighted_cols(gauss, weights):
    def block(b, total):
        row = weights[pl.ds(b, 1), :]
        for g, at in groups(b):
            total = total + gauss[at, :] * column(row, g)
        return total

    total = lax.fori_loop(0, RB, block, jnp.zeros((SUB, COLS), F32))
    return jnp.sum(total, axis=0, keepdims=True)


def weighted_rows(gauss, weights, part):
    def block(b, carry):
        acc = jnp.zeros((SUB, LANES), F32)
        for g, at in groups(b):
            acc = place(acc, jnp.sum(fold(gauss[at, :] * weights), axis=1, keepdims=True), g)
        part[pl.ds(b, 1), :] = jnp.sum(acc, axis=0, keepdims=True)
        return carry

    lax.fori_loop(0, RB, block, 0)


def first_col_kernel(logits, before, parts, weight, peak, gauss, row_scale, col_shift, part, pot):
    del before
    pot[...] = jnp.log(weight[...]) - log_sum(parts[...])
    row_scale[...] = jnp.exp(peak[...] + pot[...])
    total = weighted_cols(gauss, row_scale)
    col_shift[...] = jnp.zeros((CB, LANES), F32)
    put_dense(part, jnp.log(total))

    @pl.when(jnp.min(total) < 1e-20)
    def _():
        def shift_block(b, top):
            row = pot[pl.ds(b, 1), :]
            for g, at in groups(b):
                x = logits[at, :] + column(row, g)
                gauss[at, :] = x
                top = jnp.maximum(top, x)
            return top

        top = lax.fori_loop(0, RB, shift_block, jnp.full((SUB, COLS), -jnp.inf, F32))
        top = jnp.max(top, axis=0, keepdims=True)
        wide = jnp.broadcast_to(top, (SUB, COLS))

        def exp_block(b, total):
            for g, at in groups(b):
                x = jnp.exp(gauss[at, :] - wide)
                gauss[at, :] = x
                total = total + x
            return total

        total = lax.fori_loop(0, RB, exp_block, jnp.zeros((SUB, COLS), F32))
        row_scale[...] = jnp.ones((RB, LANES), F32)
        put_dense(col_shift, top)
        put_dense(part, top + jnp.log(jnp.sum(total, axis=0, keepdims=True)))


def first_row_kernel(gauss, parts, caps, row_scale, col_shift, part, col_scale):
    pot = jnp.log(caps[...].astype(F32)) - log_sum(parts[...])
    col_scale[...] = jnp.exp(col_shift[...] + pot)
    weighted_rows(gauss, long_row(col_scale[...]), part)
    part[...] = part[...] * row_scale[...]


def row_kernel(gauss, parts, caps, row_scale, col_scale, part):
    v = caps[...].astype(F32) / jnp.sum(parts[:, :CB], axis=0)
    weighted_rows(gauss, long_row(v * col_scale[...]), part)
    part[...] = part[...] * row_scale[...]


def col_kernel(gauss, parts, weight, row_scale, col_scale, part, u):
    rows = jnp.sum(parts[...], axis=0)
    u[...] = weight[...] / rows * row_scale[...]
    put_dense(part, weighted_cols(gauss, u))
    part[:CB, :] = part[:CB, :] * col_scale[...]
    part[CB:, :] = jnp.broadcast_to(jnp.sum(rows), (SUB, LANES))


def last_col_kernel(gauss, parts, weight, row_scale, col_scale, scaled, part, u):
    u[...] = weight[...] / jnp.sum(parts[...], axis=0) * row_scale[...]

    def block(half):
        def body(b, total):
            row = u[pl.ds(8 * half + b, 1), :]
            for g, at in groups(8 * half + b):
                i, r = g // 4, g % 4
                a = 8 * i + b if half == 0 else 4 * b + i
                value = gauss[at, :] * column(row, g)
                scaled[pl.ds(pl.multiple_of(a * 64 + 32 * half + SUB * r, SUB), SUB), :] = value
                total = total + value
            return total

        return body

    total = lax.fori_loop(0, 8, block(0), jnp.zeros((SUB, COLS), F32))
    total = lax.fori_loop(0, 8, block(1), total)
    put_dense(part, jnp.sum(total, axis=0, keepdims=True))
    part[...] = part[...] * col_scale[...]


def plan_kernel(scaled, parts, total_parts, caps, col_scale, plan, buffer, sems):
    cap_total = jnp.sum(total_parts[:, CB:], axis=0)
    factor = float(SLOTS * ASSETS) / cap_total
    v = long_row(caps[...].astype(F32) / jnp.sum(parts[...], axis=0) * col_scale[...] * factor)

    def copy(b):
        rows = pl.ds(pl.multiple_of(b * LANES, LANES), LANES)
        return pltpu.make_async_copy(buffer.at[rows], plan.at[rows], sems.at[b])

    def block(b, carry):
        for g, at in groups(b):
            buffer[at, :] = scaled[at, :] * v
        copy(b).start()
        return carry

    def wait(b, carry):
        copy(b).wait()
        return carry

    lax.fori_loop(0, RB, block, 0)
    lax.fori_loop(0, RB, wait, 0)


def call(kernel, out_shape, scratch=(), **kwargs):
    return pl.pallas_call(
        kernel,
        out_shape=out_shape,
        scratch_shapes=list(scratch),
        compiler_params=pltpu.CompilerParams(vmem_limit_bytes=VMEM_LIMIT),
        **kwargs,
    )


def in_vmem(value):
    return pltpu.with_memory_space_constraint(value, pltpu.VMEM)


def in_hbm(value):
    return pltpu.with_memory_space_constraint(value, pltpu.HBM)


VM = pl.BlockSpec(memory_space=pltpu.VMEM)


def small(rows):
    return jax.ShapeDtypeStruct((rows, LANES), F32)


def per_device(slot_emb, asset_panel, mult, caps):
    mult = mult.reshape(RB, LANES)
    caps = caps.reshape(CB, LANES)

    panels, panel_names = [shift(asset_panel, "c", 1)], [(0, 1)]
    for steps in (1, 3, 2):
        piece = shift(asset_panel, "y", steps)
        panels += [piece, shift(piece, "c", 1)]
        panel_names += [(steps, 0), (steps, 1)]

    first = [slot_emb[:32]]
    first += [shift(first[0], "x", steps) for steps in (1, 2, 3)]
    first, panels[0] = lax.optimization_barrier((jnp.concatenate(first), panels[0]))
    ahead, behind = [first], [first]
    for step in range(3):
        ahead.append(shift(ahead[-1], "z", 1))
        behind.append(shift(behind[-1], "z", -1))
    second = jnp.broadcast_to(lax.optimization_barrier(slot_emb)[None, 32:], (8, 32, EMB))
    second = lax.all_to_all(second, "z", 0, 0, tiled=True).reshape(256, EMB)
    second = ring_gather(second, "x")

    block = pltpu.VMEM((ROWS, COLS), F32)

    def take(pieces):
        names = [name for name, piece in pieces]
        pieces = [piece for name, piece in pieces]
        rows = sum(p.shape[0] for p in pieces)
        scratch = [pltpu.VMEM((rows, EMB), jnp.bfloat16), pltpu.SMEM((rows // LANES,), jnp.int32)]
        cost = pl.CostEstimate(flops=2 * rows * EMB * COLS, bytes_accessed=rows * 8192, transcendentals=rows * COLS)
        return names, pieces, scratch, cost

    def some(kind, k):
        if kind == "x":
            return [(("x", k, i), piece) for i, piece in enumerate(second[k])]
        if k == 4:
            return [(("z", 4, 0), shift(ahead[3][:64], "z", 1)), (("z", 4, 2), shift(behind[3][64:], "z", -1))]
        return [(("z", k, 0), ahead[k] if k < 4 else behind[8 - k])]

    names, pieces, scratch, cost = take(some("z", 0) + some("z", 1) + some("x", 0))
    hbm = pl.BlockSpec(memory_space=pltpu.HBM)
    logits, gauss, peak, part, panel, weight = call(
        functools.partial(first_kernel, panel_names, names),
        (block, block, small(RB), small(RB), pltpu.VMEM((EMB, COLS), jnp.bfloat16), small(RB)),
        in_specs=[hbm, hbm] + [VM] * (len(panels) + len(pieces)),
        out_specs=(VM,) * 6,
        scratch=scratch + [pltpu.VMEM((RB, LANES), jnp.int32), pltpu.SemaphoreType.DMA((2,))],
        cost_estimate=cost,
    )(in_hbm(asset_panel), in_hbm(mult), *panels, *pieces)
    ahead[3], behind[3], part = lax.optimization_barrier((ahead[3], behind[3], part))
    middle = some("z", 7) + some("z", 2) + some("z", 6) + some("z", 3) + some("x", 1) + some("x", 3)
    last = some("z", 5) + some("z", 4) + some("x", 2)
    for pieces in (middle, last):
        names, pieces, scratch, cost = take(pieces)
        logits, gauss, peak, part = call(
            functools.partial(more_kernel, names),
            (block, block, small(RB), small(RB)),
            in_specs=[VM] * (5 + len(pieces)),
            out_specs=(VM,) * 4,
            scratch=scratch,
            input_output_aliases={0: 0, 1: 1, 2: 2, 3: 3},
            cost_estimate=cost,
        )(in_vmem(logits), in_vmem(gauss), peak, part, in_vmem(panel), *pieces)

    gauss, row_scale, col_shift, part = call(
        first_col_kernel,
        (block, small(RB), small(CB), small(CB)),
        in_specs=[VM] * 5,
        out_specs=(VM,) * 4,
        scratch=[pltpu.VMEM((RB, LANES), F32)],
        input_output_aliases={1: 0},
    )(in_vmem(logits), in_vmem(gauss), over_asset(part), weight, peak)
    part, col_scale = call(first_row_kernel, (small(RB), small(CB)), in_specs=[VM] * 5, out_specs=(VM, VM))(
        in_vmem(gauss), over_slot(part), caps, row_scale, col_shift
    )
    u_space = [pltpu.VMEM((RB, LANES), F32)]
    for iteration in range(1, ITERS - 1):
        part = call(col_kernel, small(CB + SUB), in_specs=[VM] * 5, out_specs=VM, scratch=u_space)(
            in_vmem(gauss), over_asset(part), weight, row_scale, col_scale
        )
        total_parts = over_slot(part)
        part = call(row_kernel, small(RB), in_specs=[VM] * 5, out_specs=VM)(
            in_vmem(gauss), total_parts, caps, row_scale, col_scale
        )
    scaled, part = call(last_col_kernel, (block, small(CB)), in_specs=[VM] * 5, out_specs=(VM, VM), scratch=u_space)(
        in_vmem(gauss), over_asset(part), weight, row_scale, col_scale
    )
    return call(
        plan_kernel,
        jax.ShapeDtypeStruct((ROWS, COLS), F32),
        in_specs=[VM] * 5,
        out_specs=pl.BlockSpec(memory_space=pltpu.HBM),
        scratch=[pltpu.VMEM((ROWS, COLS), F32), pltpu.SemaphoreType.DMA((RB,))],
    )(in_vmem(scaled), over_slot(part), total_parts, caps, col_scale)


def solution(mesh):
    fine = Mesh(mesh.devices.reshape(4, 2, 4, 8), ("y", "c", "x", "z"))
    slot, asset = ("y", "c"), ("x", "z")
    return jax.shard_map(
        per_device,
        mesh=fine,
        in_specs=(P(slot + asset, None), P(slot, asset), P(slot), P(asset)),
        out_specs=P(slot, asset),
        check_vma=False,
    )
```

```python
import functools

import jax
import jax.numpy as jnp
from jax import lax
from jax.experimental import pallas as pl
from jax.experimental.pallas import tpu as pltpu
from jax.sharding import Mesh, PartitionSpec as P

EMB = 768
ITERS = 3
SLOTS = 16384
ASSETS = 32768
ROWS, COLS = 2048, 1024
LANES, SUB = 128, 8
RB, CB = ROWS // LANES, COLS // LANES
VMEM_LIMIT = 28 << 20
BLOCK = 512
F32 = jnp.float32


def shift(value, axis, step):
    size = lax.axis_size(axis)
    return lax.ppermute(value, axis, [(i, (i + step) % size) for i in range(size)])


def ring_gather(value, axis):
    size = lax.axis_size(axis)
    shards = {0: [value]}
    ahead = behind = value
    for step in range(1, size // 2):
        ahead = shift(ahead, axis, 1)
        behind = shift(behind, axis, -1)
        shards[step] = [ahead]
        shards[size - step] = [behind]
    half = value.shape[0] // 2
    shards[size // 2] = [shift(ahead[:half], axis, 1), shift(behind[half:], axis, -1)]
    return shards


def over_asset(part):
    copies = jnp.broadcast_to(part[None], (32,) + part.shape)
    return lax.all_to_all(copies, ("x", "z"), 0, 0, tiled=True)


def over_slot(part):
    copies = jnp.broadcast_to(part[None], (8,) + part.shape)
    return lax.all_to_all(copies, ("y", "c"), 0, 0, tiled=True)


def iotas():
    lane = lax.broadcasted_iota(jnp.int32, (SUB, LANES), 1)
    row = lax.broadcasted_iota(jnp.int32, (SUB, LANES), 0)
    return lane, row


def column(row, g):
    lane, sub = iotas()
    return jnp.sum(jnp.where(lane == sub + SUB * g, row, 0.0), axis=1, keepdims=True)


def place(acc, col, g):
    lane, sub = iotas()
    return jnp.where(lane == sub + SUB * g, col, acc)


def long_row(dense):
    row = jnp.concatenate([dense[k : k + 1, :] for k in range(CB)], axis=1)
    return jnp.broadcast_to(row, (SUB, COLS))


def put_dense(ref, row):
    for k in range(CB):
        ref[k : k + 1, :] = row[:, LANES * k : LANES * (k + 1)]


def fold(wide):
    total = wide[:, :LANES]
    for k in range(1, CB):
        total = total + wide[:, LANES * k : LANES * (k + 1)]
    return total


def log_sum(parts):
    peak = jnp.max(parts, axis=0)
    return peak + jnp.log(jnp.sum(jnp.exp(parts - peak[None]), axis=0))


def groups(b):
    for g in range(LANES // SUB):
        yield g, pl.ds(pl.multiple_of(b * LANES + SUB * g, SUB), SUB)


def row_stats(value, gauss, peak, part, unit):
    peaks = []
    for g in range(LANES // SUB):
        x = value[SUB * g : SUB * (g + 1), :]
        wide = x[:, :LANES]
        for k in range(1, CB):
            wide = jnp.maximum(wide, x[:, LANES * k : LANES * (k + 1)])
        peaks.append(jnp.max(wide, axis=1, keepdims=True))
    peak_row = jnp.zeros((SUB, LANES), F32)
    total_row = jnp.zeros((SUB, LANES), F32)
    for g, at in groups(unit):
        x = jnp.exp(value[SUB * g : SUB * (g + 1), :] - peaks[g])
        gauss[at, :] = x
        total_row = place(total_row, jnp.sum(fold(x), axis=1, keepdims=True), g)
        peak_row = place(peak_row, peaks[g], g)
    peak_row = jnp.sum(peak_row, axis=0, keepdims=True)
    peak[pl.ds(unit, 1), :] = peak_row
    part[pl.ds(unit, 1), :] = peak_row + jnp.log(jnp.sum(total_row, axis=0, keepdims=True))


def block_logits(slot, panel, outs, table, count):
    logits = outs[0]
    units = BLOCK // LANES

    def block(b, carry):
        for t in range(units):
            rows = pl.ds(pl.multiple_of(b * BLOCK + t * LANES, LANES), LANES)
            value = jnp.dot(slot[rows, :], panel[...], preferred_element_type=F32) * EMB ** (-0.5)
            unit = table[b * units + t]
            logits[pl.ds(pl.multiple_of(unit * LANES, LANES), LANES), :] = value
            row_stats(value, *outs[1:], unit)
        return carry

    lax.fori_loop(0, count // BLOCK, block, 0)


def back(axis, steps):
    size = lax.axis_size(axis)
    return lax.rem(lax.axis_index(axis) - steps + size, size)


def put_slots(pieces, names, slot, table):
    at = 0
    for ref, (axis, steps, offset) in zip(pieces, names):
        rows = ref.shape[0]
        unit = at // LANES
        if axis == "z":
            table[unit] = back("z", steps)
            for j in range(rows // 32):
                to = pl.multiple_of(unit * LANES + back("x", offset + j) * 32, 32)
                slot[pl.ds(to, 32), :] = ref[32 * j : 32 * (j + 1), :]
        else:
            slot[at : at + rows, :] = ref[...]
            for i in range(rows // LANES):
                table[unit + i] = 8 + 2 * back("x", steps) + offset + i
        at += rows


def reorder_mult(mult):
    value = mult.astype(F32)
    lane, _ = iotas()
    rolled = [value] + [pltpu.roll(value, 32 * k, axis=1) for k in (1, 2, 3)]

    def moved(row, block, to):
        return rolled[(to - block) % 4][row : row + 1, :]

    def merged(pieces):
        out = pieces[0]
        for k in (1, 2, 3):
            out = jnp.where(lane[:1] >= 32 * k, pieces[k], out)
        return out

    rows = [merged([moved(4 * x + z // 2, 2 * (z % 2), x) for x in range(4)]) for z in range(8)]
    for x in range(4):
        for top in range(2):
            rows.append(merged([moved(4 * x + 2 * top + i // 2, 2 * (i % 2) + 1, i) for i in range(4)]))
    return rows


def first_kernel(panel_names, slot_names, *refs):
    n, m = len(panel_names), len(slot_names)
    own, mult, panels, slots = refs[0], refs[1], refs[2 : 2 + n], refs[2 + n : 2 + n + m]
    *outs, panel, weight, slot, table, raw, sems = refs[2 + n + m :]
    at = pl.ds(pl.multiple_of((back("y", 0) * 2 + back("c", 0)) * 96, 32), 96)
    copy = pltpu.make_async_copy(own, panel.at[at], sems.at[0])
    copy.start()
    small_copy = pltpu.make_async_copy(mult, raw, sems.at[1])
    small_copy.start()
    for ref, (y_steps, c_steps) in zip(panels, panel_names):
        start = (back("y", y_steps) * 2 + back("c", c_steps)) * 96
        panel[pl.ds(pl.multiple_of(start, 32), 96), :] = ref[...]
    put_slots(slots, slot_names, slot, table)
    small_copy.wait()
    for i, row in enumerate(reorder_mult(raw[...])):
        weight[i : i + 1, :] = row
    copy.wait()
    block_logits(slot, panel, outs, table, slot.shape[0])


def more_kernel(slot_names, logits, gauss, peak, part, panel, *refs):
    m = len(slot_names)
    del logits, gauss, peak, part
    slots, (*outs, slot, table) = refs[:m], refs[m:]
    put_slots(slots, slot_names, slot, table)
    block_logits(slot, panel, outs, table, slot.shape[0])


def weighted_cols(gauss, weights):
    def block(b, total):
        row = weights[pl.ds(b, 1), :]
        for g, at in groups(b):
            total = total + gauss[at, :] * column(row, g)
        return total

    total = lax.fori_loop(0, RB, block, jnp.zeros((SUB, COLS), F32))
    return jnp.sum(total, axis=0, keepdims=True)


def weighted_rows(gauss, weights, part):
    def block(b, carry):
        acc = jnp.zeros((SUB, LANES), F32)
        for g, at in groups(b):
            acc = place(acc, jnp.sum(fold(gauss[at, :] * weights), axis=1, keepdims=True), g)
        part[pl.ds(b, 1), :] = jnp.sum(acc, axis=0, keepdims=True)
        return carry

    lax.fori_loop(0, RB, block, 0)


def first_col_kernel(logits, before, parts, weight, peak, gauss, row_scale, col_shift, part, pot):
    del before
    pot[...] = jnp.log(weight[...]) - log_sum(parts[...])
    row_scale[...] = jnp.exp(peak[...] + pot[...])
    total = weighted_cols(gauss, row_scale)
    col_shift[...] = jnp.zeros((CB, LANES), F32)
    put_dense(part, jnp.log(total))

    @pl.when(jnp.min(total) < 1e-20)
    def _():
        def shift_block(b, top):
            row = pot[pl.ds(b, 1), :]
            for g, at in groups(b):
                x = logits[at, :] + column(row, g)
                gauss[at, :] = x
                top = jnp.maximum(top, x)
            return top

        top = lax.fori_loop(0, RB, shift_block, jnp.full((SUB, COLS), -jnp.inf, F32))
        top = jnp.max(top, axis=0, keepdims=True)
        wide = jnp.broadcast_to(top, (SUB, COLS))

        def exp_block(b, total):
            for g, at in groups(b):
                x = jnp.exp(gauss[at, :] - wide)
                gauss[at, :] = x
                total = total + x
            return total

        total = lax.fori_loop(0, RB, exp_block, jnp.zeros((SUB, COLS), F32))
        row_scale[...] = jnp.ones((RB, LANES), F32)
        put_dense(col_shift, top)
        put_dense(part, top + jnp.log(jnp.sum(total, axis=0, keepdims=True)))


def first_row_kernel(gauss, parts, caps, row_scale, col_shift, part, col_scale):
    pot = jnp.log(caps[...].astype(F32)) - log_sum(parts[...])
    col_scale[...] = jnp.exp(col_shift[...] + pot)
    weighted_rows(gauss, long_row(col_scale[...]), part)
    part[...] = part[...] * row_scale[...]


def row_kernel(gauss, parts, caps, row_scale, col_scale, part):
    v = caps[...].astype(F32) / jnp.sum(parts[:, :CB], axis=0)
    weighted_rows(gauss, long_row(v * col_scale[...]), part)
    part[...] = part[...] * row_scale[...]


def col_kernel(gauss, parts, weight, row_scale, col_scale, part, u):
    rows = jnp.sum(parts[...], axis=0)
    u[...] = weight[...] / rows * row_scale[...]
    put_dense(part, weighted_cols(gauss, u))
    part[:CB, :] = part[:CB, :] * col_scale[...]
    part[CB:, :] = jnp.broadcast_to(jnp.sum(rows), (SUB, LANES))


def last_col_kernel(gauss, parts, weight, row_scale, col_scale, scaled, part, u):
    u[...] = weight[...] / jnp.sum(parts[...], axis=0) * row_scale[...]

    def block(half):
        def body(b, total):
            row = u[pl.ds(8 * half + b, 1), :]
            for g, at in groups(8 * half + b):
                i, r = g // 4, g % 4
                a = 8 * i + b if half == 0 else 4 * b + i
                value = gauss[at, :] * column(row, g)
                scaled[pl.ds(pl.multiple_of(a * 64 + 32 * half + SUB * r, SUB), SUB), :] = value
                total = total + value
            return total

        return body

    total = lax.fori_loop(0, 8, block(0), jnp.zeros((SUB, COLS), F32))
    total = lax.fori_loop(0, 8, block(1), total)
    put_dense(part, jnp.sum(total, axis=0, keepdims=True))
    part[...] = part[...] * col_scale[...]


def plan_kernel(scaled, parts, total_parts, caps, col_scale, plan, buffer, sems):
    cap_total = jnp.sum(total_parts[:, CB:], axis=0)
    factor = float(SLOTS * ASSETS) / cap_total
    v = long_row(caps[...].astype(F32) / jnp.sum(parts[...], axis=0) * col_scale[...] * factor)

    def copy(b):
        rows = pl.ds(pl.multiple_of(b * LANES, LANES), LANES)
        return pltpu.make_async_copy(buffer.at[rows], plan.at[rows], sems.at[b])

    def block(b, carry):
        for g, at in groups(b):
            buffer[at, :] = scaled[at, :] * v
        copy(b).start()
        return carry

    def wait(b, carry):
        copy(b).wait()
        return carry

    lax.fori_loop(0, RB, block, 0)
    lax.fori_loop(0, RB, wait, 0)


def call(kernel, out_shape, scratch=(), **kwargs):
    return pl.pallas_call(
        kernel,
        out_shape=out_shape,
        scratch_shapes=list(scratch),
        compiler_params=pltpu.CompilerParams(vmem_limit_bytes=VMEM_LIMIT),
        **kwargs,
    )


def in_vmem(value):
    return pltpu.with_memory_space_constraint(value, pltpu.VMEM)


def in_hbm(value):
    return pltpu.with_memory_space_constraint(value, pltpu.HBM)


VM = pl.BlockSpec(memory_space=pltpu.VMEM)


def small(rows):
    return jax.ShapeDtypeStruct((rows, LANES), F32)


def per_device(slot_emb, asset_panel, mult, caps):
    mult = mult.reshape(RB, LANES)
    caps = caps.reshape(CB, LANES)

    panels, panel_names = [shift(asset_panel, "c", 1)], [(0, 1)]
    for steps in (1, 3, 2):
        piece = shift(asset_panel, "y", steps)
        panels += [piece, shift(piece, "c", 1)]
        panel_names += [(steps, 0), (steps, 1)]

    first = [slot_emb[:32]]
    first += [shift(first[0], "x", steps) for steps in (1, 2, 3)]
    first = jnp.concatenate(first)
    ahead, behind = [first], [first]
    for step in range(3):
        ahead.append(shift(ahead[-1], "z", 1))
        behind.append(shift(behind[-1], "z", -1))
    second = jnp.broadcast_to(slot_emb[None, 32:], (8, 32, EMB))
    second = lax.all_to_all(second, "z", 0, 0, tiled=True).reshape(256, EMB)
    second = ring_gather(second, "x")

    block = pltpu.VMEM((ROWS, COLS), F32)

    def take(pieces):
        names = [name for name, piece in pieces]
        pieces = [piece for name, piece in pieces]
        rows = sum(p.shape[0] for p in pieces)
        scratch = [pltpu.VMEM((rows, EMB), jnp.bfloat16), pltpu.SMEM((rows // LANES,), jnp.int32)]
        cost = pl.CostEstimate(flops=2 * rows * EMB * COLS, bytes_accessed=rows * 8192, transcendentals=rows * COLS)
        return names, pieces, scratch, cost

    def some(kind, k):
        if kind == "x":
            return [(("x", k, i), piece) for i, piece in enumerate(second[k])]
        if k == 4:
            return [(("z", 4, 0), shift(ahead[3][:64], "z", 1)), (("z", 4, 2), shift(behind[3][64:], "z", -1))]
        return [(("z", k, 0), ahead[k] if k < 4 else behind[8 - k])]

    names, pieces, scratch, cost = take(some("z", 0) + some("z", 1) + some("x", 0))
    hbm = pl.BlockSpec(memory_space=pltpu.HBM)
    logits, gauss, peak, part, panel, weight = call(
        functools.partial(first_kernel, panel_names, names),
        (block, block, small(RB), small(RB), pltpu.VMEM((EMB, COLS), jnp.bfloat16), small(RB)),
        in_specs=[hbm, hbm] + [VM] * (len(panels) + len(pieces)),
        out_specs=(VM,) * 6,
        scratch=scratch + [pltpu.VMEM((RB, LANES), jnp.int32), pltpu.SemaphoreType.DMA((2,))],
        cost_estimate=cost,
    )(in_hbm(asset_panel), in_hbm(mult), *panels, *pieces)
    ahead[3], behind[3], part = lax.optimization_barrier((ahead[3], behind[3], part))
    middle = some("z", 7) + some("z", 2) + some("z", 6) + some("z", 3) + some("x", 1) + some("x", 3)
    last = some("z", 5) + some("z", 4) + some("x", 2)
    for pieces in (middle, last):
        names, pieces, scratch, cost = take(pieces)
        logits, gauss, peak, part = call(
            functools.partial(more_kernel, names),
            (block, block, small(RB), small(RB)),
            in_specs=[VM] * (5 + len(pieces)),
            out_specs=(VM,) * 4,
            scratch=scratch,
            input_output_aliases={0: 0, 1: 1, 2: 2, 3: 3},
            cost_estimate=cost,
        )(in_vmem(logits), in_vmem(gauss), peak, part, in_vmem(panel), *pieces)

    gauss, row_scale, col_shift, part = call(
        first_col_kernel,
        (block, small(RB), small(CB), small(CB)),
        in_specs=[VM] * 5,
        out_specs=(VM,) * 4,
        scratch=[pltpu.VMEM((RB, LANES), F32)],
        input_output_aliases={1: 0},
    )(in_vmem(logits), in_vmem(gauss), over_asset(part), weight, peak)
    part, col_scale = call(first_row_kernel, (small(RB), small(CB)), in_specs=[VM] * 5, out_specs=(VM, VM))(
        in_vmem(gauss), over_slot(part), caps, row_scale, col_shift
    )
    u_space = [pltpu.VMEM((RB, LANES), F32)]
    for iteration in range(1, ITERS - 1):
        part = call(col_kernel, small(CB + SUB), in_specs=[VM] * 5, out_specs=VM, scratch=u_space)(
            in_vmem(gauss), over_asset(part), weight, row_scale, col_scale
        )
        total_parts = over_slot(part)
        part = call(row_kernel, small(RB), in_specs=[VM] * 5, out_specs=VM)(
            in_vmem(gauss), total_parts, caps, row_scale, col_scale
        )
    scaled, part = call(last_col_kernel, (block, small(CB)), in_specs=[VM] * 5, out_specs=(VM, VM), scratch=u_space)(
        in_vmem(gauss), over_asset(part), weight, row_scale, col_scale
    )
    return call(
        plan_kernel,
        jax.ShapeDtypeStruct((ROWS, COLS), F32),
        in_specs=[VM] * 5,
        out_specs=pl.BlockSpec(memory_space=pltpu.HBM),
        scratch=[pltpu.VMEM((ROWS, COLS), F32), pltpu.SemaphoreType.DMA((RB,))],
    )(in_vmem(scaled), over_slot(part), total_parts, caps, col_scale)


def solution(mesh):
    fine = Mesh(mesh.devices.reshape(4, 2, 4, 8), ("y", "c", "x", "z"))
    slot, asset = ("y", "c"), ("x", "z")
    return jax.shard_map(
        per_device,
        mesh=fine,
        in_specs=(P(slot + asset, None), P(slot, asset), P(slot), P(asset)),
        out_specs=P(slot, asset),
        check_vma=False,
    )
```

```python
import functools

import jax
import jax.numpy as jnp
from jax import lax
from jax.experimental import pallas as pl
from jax.experimental.pallas import tpu as pltpu
from jax.sharding import Mesh, PartitionSpec as P

EMB = 768
ITERS = 3
SLOTS = 16384
ASSETS = 32768
ROWS, COLS = 2048, 1024
LANES, SUB = 128, 8
RB, CB = ROWS // LANES, COLS // LANES
VMEM_LIMIT = 28 << 20
BLOCK = 512
F32 = jnp.float32


def shift(value, axis, step):
    size = lax.axis_size(axis)
    return lax.ppermute(value, axis, [(i, (i + step) % size) for i in range(size)])


def over_asset(part):
    copies = jnp.broadcast_to(part[None], (32,) + part.shape)
    return lax.all_to_all(copies, ("x", "z"), 0, 0, tiled=True)


def over_slot(part):
    copies = jnp.broadcast_to(part[None], (8,) + part.shape)
    return lax.all_to_all(copies, ("y", "c"), 0, 0, tiled=True)


def iotas():
    lane = lax.broadcasted_iota(jnp.int32, (SUB, LANES), 1)
    row = lax.broadcasted_iota(jnp.int32, (SUB, LANES), 0)
    return lane, row


def column(row, g):
    lane, sub = iotas()
    return jnp.sum(jnp.where(lane == sub + SUB * g, row, 0.0), axis=1, keepdims=True)


def place(acc, col, g):
    lane, sub = iotas()
    return jnp.where(lane == sub + SUB * g, col, acc)


def long_row(dense):
    row = jnp.concatenate([dense[k : k + 1, :] for k in range(CB)], axis=1)
    return jnp.broadcast_to(row, (SUB, COLS))


def put_dense(ref, row):
    for k in range(CB):
        ref[k : k + 1, :] = row[:, LANES * k : LANES * (k + 1)]


def fold(wide):
    total = wide[:, :LANES]
    for k in range(1, CB):
        total = total + wide[:, LANES * k : LANES * (k + 1)]
    return total


def log_sum(parts):
    peak = jnp.max(parts, axis=0)
    return peak + jnp.log(jnp.sum(jnp.exp(parts - peak[None]), axis=0))


def groups(b):
    for g in range(LANES // SUB):
        yield g, pl.ds(pl.multiple_of(b * LANES + SUB * g, SUB), SUB)


def row_stats(value, gauss, peak, part, unit):
    peaks = []
    for g in range(LANES // SUB):
        x = value[SUB * g : SUB * (g + 1), :]
        wide = x[:, :LANES]
        for k in range(1, CB):
            wide = jnp.maximum(wide, x[:, LANES * k : LANES * (k + 1)])
        peaks.append(jnp.max(wide, axis=1, keepdims=True))
    peak_row = jnp.zeros((SUB, LANES), F32)
    total_row = jnp.zeros((SUB, LANES), F32)
    for g, at in groups(unit):
        x = jnp.exp(value[SUB * g : SUB * (g + 1), :] - peaks[g])
        gauss[at, :] = x
        total_row = place(total_row, jnp.sum(fold(x), axis=1, keepdims=True), g)
        peak_row = place(peak_row, peaks[g], g)
    peak_row = jnp.sum(peak_row, axis=0, keepdims=True)
    peak[pl.ds(unit, 1), :] = peak_row
    part[pl.ds(unit, 1), :] = peak_row + jnp.log(jnp.sum(total_row, axis=0, keepdims=True))


def block_logits(slot, panel, outs, table, count):
    logits = outs[0]
    units = BLOCK // LANES

    def block(b, carry):
        for t in range(units):
            rows = pl.ds(pl.multiple_of(b * BLOCK + t * LANES, LANES), LANES)
            value = jnp.dot(slot[rows, :], panel[...], preferred_element_type=F32) * EMB ** (-0.5)
            unit = table[b * units + t]
            logits[pl.ds(pl.multiple_of(unit * LANES, LANES), LANES), :] = value
            row_stats(value, *outs[1:], unit)
        return carry

    lax.fori_loop(0, count // BLOCK, block, 0)


def back(axis, steps):
    size = lax.axis_size(axis)
    return lax.rem(lax.axis_index(axis) - steps + size, size)


def put_slots(pieces, names, slot, table):
    at = 0
    for ref, (axis, steps, offset) in zip(pieces, names):
        rows = ref.shape[0]
        unit = at // LANES
        if axis == "z":
            table[unit] = back("z", steps)
            for j in range(rows // 32):
                to = pl.multiple_of(unit * LANES + back("x", offset + j) * 32, 32)
                slot[pl.ds(to, 32), :] = ref[32 * j : 32 * (j + 1), :]
        else:
            slot[at : at + rows, :] = ref[...]
            for i in range(rows // LANES):
                table[unit + i] = 8 + 2 * back("x", steps) + offset + i
        at += rows


def reorder_mult(mult):
    value = mult.astype(F32)
    lane, _ = iotas()
    rolled = [value] + [pltpu.roll(value, 32 * k, axis=1) for k in (1, 2, 3)]

    def moved(row, block, to):
        return rolled[(to - block) % 4][row : row + 1, :]

    def merged(pieces):
        out = pieces[0]
        for k in (1, 2, 3):
            out = jnp.where(lane[:1] >= 32 * k, pieces[k], out)
        return out

    rows = [merged([moved(4 * x + z // 2, 2 * (z % 2), x) for x in range(4)]) for z in range(8)]
    for x in range(4):
        for top in range(2):
            rows.append(merged([moved(4 * x + 2 * top + i // 2, 2 * (i % 2) + 1, i) for i in range(4)]))
    return rows


def first_kernel(panel_names, slot_names, *refs):
    n, m = len(panel_names), len(slot_names)
    own, mult, panels, slots = refs[0], refs[1], refs[2 : 2 + n], refs[2 + n : 2 + n + m]
    *outs, panel, weight, slot, table, raw, sems = refs[2 + n + m :]
    at = pl.ds(pl.multiple_of((back("y", 0) * 2 + back("c", 0)) * 96, 32), 96)
    copy = pltpu.make_async_copy(own, panel.at[at], sems.at[0])
    copy.start()
    small_copy = pltpu.make_async_copy(mult, raw, sems.at[1])
    small_copy.start()
    for ref, (y_steps, c_steps) in zip(panels, panel_names):
        start = (back("y", y_steps) * 2 + back("c", c_steps)) * 96
        panel[pl.ds(pl.multiple_of(start, 32), 96), :] = ref[...]
    put_slots(slots, slot_names, slot, table)
    small_copy.wait()
    for i, row in enumerate(reorder_mult(raw[...])):
        weight[i : i + 1, :] = row
    copy.wait()
    block_logits(slot, panel, outs, table, slot.shape[0])


def more_kernel(slot_names, logits, gauss, peak, part, panel, *refs):
    m = len(slot_names)
    del logits, gauss, peak, part
    slots, (*outs, slot, table) = refs[:m], refs[m:]
    put_slots(slots, slot_names, slot, table)
    block_logits(slot, panel, outs, table, slot.shape[0])


def weighted_cols(gauss, weights):
    def block(b, total):
        row = weights[pl.ds(b, 1), :]
        for g, at in groups(b):
            total = total + gauss[at, :] * column(row, g)
        return total

    total = lax.fori_loop(0, RB, block, jnp.zeros((SUB, COLS), F32))
    return jnp.sum(total, axis=0, keepdims=True)


def weighted_rows(gauss, weights, part):
    def block(b, carry):
        acc = jnp.zeros((SUB, LANES), F32)
        for g, at in groups(b):
            acc = place(acc, jnp.sum(fold(gauss[at, :] * weights), axis=1, keepdims=True), g)
        part[pl.ds(b, 1), :] = jnp.sum(acc, axis=0, keepdims=True)
        return carry

    lax.fori_loop(0, RB, block, 0)


def first_col_kernel(logits, before, parts, weight, peak, gauss, row_scale, col_shift, part, pot):
    del before
    pot[...] = jnp.log(weight[...]) - log_sum(parts[...])
    row_scale[...] = jnp.exp(peak[...] + pot[...])
    total = weighted_cols(gauss, row_scale)
    col_shift[...] = jnp.zeros((CB, LANES), F32)
    put_dense(part, jnp.log(total))

    @pl.when(jnp.min(total) < 1e-20)
    def _():
        def shift_block(b, top):
            row = pot[pl.ds(b, 1), :]
            for g, at in groups(b):
                x = logits[at, :] + column(row, g)
                gauss[at, :] = x
                top = jnp.maximum(top, x)
            return top

        top = lax.fori_loop(0, RB, shift_block, jnp.full((SUB, COLS), -jnp.inf, F32))
        top = jnp.max(top, axis=0, keepdims=True)
        wide = jnp.broadcast_to(top, (SUB, COLS))

        def exp_block(b, total):
            for g, at in groups(b):
                x = jnp.exp(gauss[at, :] - wide)
                gauss[at, :] = x
                total = total + x
            return total

        total = lax.fori_loop(0, RB, exp_block, jnp.zeros((SUB, COLS), F32))
        row_scale[...] = jnp.ones((RB, LANES), F32)
        put_dense(col_shift, top)
        put_dense(part, top + jnp.log(jnp.sum(total, axis=0, keepdims=True)))


def first_row_kernel(gauss, parts, caps, row_scale, col_shift, part, col_scale):
    pot = jnp.log(caps[...].astype(F32)) - log_sum(parts[...])
    col_scale[...] = jnp.exp(col_shift[...] + pot)
    weighted_rows(gauss, long_row(col_scale[...]), part)
    part[...] = part[...] * row_scale[...]


def row_kernel(gauss, parts, caps, row_scale, col_scale, part):
    v = caps[...].astype(F32) / jnp.sum(parts[:, :CB], axis=0)
    weighted_rows(gauss, long_row(v * col_scale[...]), part)
    part[...] = part[...] * row_scale[...]


def col_kernel(gauss, parts, weight, row_scale, col_scale, part, u):
    rows = jnp.sum(parts[...], axis=0)
    u[...] = weight[...] / rows * row_scale[...]
    put_dense(part, weighted_cols(gauss, u))
    part[:CB, :] = part[:CB, :] * col_scale[...]
    part[CB:, :] = jnp.broadcast_to(jnp.sum(rows), (SUB, LANES))


def last_col_kernel(gauss, parts, weight, row_scale, col_scale, scaled, part, u):
    u[...] = weight[...] / jnp.sum(parts[...], axis=0) * row_scale[...]

    def block(half):
        def body(b, total):
            row = u[pl.ds(8 * half + b, 1), :]
            for g, at in groups(8 * half + b):
                i, r = g // 4, g % 4
                a = 8 * i + b if half == 0 else 4 * b + i
                value = gauss[at, :] * column(row, g)
                scaled[pl.ds(pl.multiple_of(a * 64 + 32 * half + SUB * r, SUB), SUB), :] = value
                total = total + value
            return total

        return body

    total = lax.fori_loop(0, 8, block(0), jnp.zeros((SUB, COLS), F32))
    total = lax.fori_loop(0, 8, block(1), total)
    put_dense(part, jnp.sum(total, axis=0, keepdims=True))
    part[...] = part[...] * col_scale[...]


def plan_kernel(scaled, parts, total_parts, caps, col_scale, plan, buffer, sems):
    cap_total = jnp.sum(total_parts[:, CB:], axis=0)
    factor = float(SLOTS * ASSETS) / cap_total
    v = long_row(caps[...].astype(F32) / jnp.sum(parts[...], axis=0) * col_scale[...] * factor)

    def copy(b):
        rows = pl.ds(pl.multiple_of(b * LANES, LANES), LANES)
        return pltpu.make_async_copy(buffer.at[rows], plan.at[rows], sems.at[b])

    def block(b, carry):
        for g, at in groups(b):
            buffer[at, :] = scaled[at, :] * v
        copy(b).start()
        return carry

    def wait(b, carry):
        copy(b).wait()
        return carry

    lax.fori_loop(0, RB, block, 0)
    lax.fori_loop(0, RB, wait, 0)


def call(kernel, out_shape, scratch=(), **kwargs):
    return pl.pallas_call(
        kernel,
        out_shape=out_shape,
        scratch_shapes=list(scratch),
        compiler_params=pltpu.CompilerParams(vmem_limit_bytes=VMEM_LIMIT),
        **kwargs,
    )


def in_vmem(value):
    return pltpu.with_memory_space_constraint(value, pltpu.VMEM)


def in_hbm(value):
    return pltpu.with_memory_space_constraint(value, pltpu.HBM)


VM = pl.BlockSpec(memory_space=pltpu.VMEM)


def small(rows):
    return jax.ShapeDtypeStruct((rows, LANES), F32)


def per_device(slot_emb, asset_panel, mult, caps):
    mult = mult.reshape(RB, LANES)
    caps = caps.reshape(CB, LANES)

    panels, panel_names = [shift(asset_panel, "c", 1)], [(0, 1)]
    for steps in (1, 3, 2):
        piece = shift(asset_panel, "y", steps)
        panels += [piece, shift(piece, "c", 1)]
        panel_names += [(steps, 0), (steps, 1)]

    first = [slot_emb[:32]]
    first += [shift(first[0], "x", steps) for steps in (1, 2, 3)]
    first = jnp.concatenate(first)
    ahead, behind = [first], [first]
    for step in range(3):
        ahead.append(shift(ahead[-1], "z", 1))
        behind.append(shift(behind[-1], "z", -1))
    second = jnp.broadcast_to(slot_emb[None, 32:], (8, 32, EMB))
    second = lax.all_to_all(second, "z", 0, 0, tiled=True).reshape(256, EMB)
    second = [[second]] + [[shift(second, "x", steps)] for steps in (1, 2, 3)]

    block = pltpu.VMEM((ROWS, COLS), F32)

    def take(pieces):
        names = [name for name, piece in pieces]
        pieces = [piece for name, piece in pieces]
        rows = sum(p.shape[0] for p in pieces)
        scratch = [pltpu.VMEM((rows, EMB), jnp.bfloat16), pltpu.SMEM((rows // LANES,), jnp.int32)]
        cost = pl.CostEstimate(flops=2 * rows * EMB * COLS, bytes_accessed=rows * 8192, transcendentals=rows * COLS)
        return names, pieces, scratch, cost

    def some(kind, k):
        if kind == "x":
            return [(("x", k, i), piece) for i, piece in enumerate(second[k])]
        if k == 4:
            return [(("z", 4, 0), shift(ahead[3][:64], "z", 1)), (("z", 4, 2), shift(behind[3][64:], "z", -1))]
        return [(("z", k, 0), ahead[k] if k < 4 else behind[8 - k])]

    names, pieces, scratch, cost = take(some("z", 0) + some("z", 1) + some("x", 0))
    hbm = pl.BlockSpec(memory_space=pltpu.HBM)
    logits, gauss, peak, part, panel, weight = call(
        functools.partial(first_kernel, panel_names, names),
        (block, block, small(RB), small(RB), pltpu.VMEM((EMB, COLS), jnp.bfloat16), small(RB)),
        in_specs=[hbm, hbm] + [VM] * (len(panels) + len(pieces)),
        out_specs=(VM,) * 6,
        scratch=scratch + [pltpu.VMEM((RB, LANES), jnp.int32), pltpu.SemaphoreType.DMA((2,))],
        cost_estimate=cost,
    )(in_hbm(asset_panel), in_hbm(mult), *panels, *pieces)
    ahead[3], behind[3], part = lax.optimization_barrier((ahead[3], behind[3], part))
    middle = some("z", 7) + some("z", 2) + some("z", 6) + some("z", 3) + some("x", 1) + some("x", 3)
    last = some("z", 5) + some("z", 4) + some("x", 2)
    for pieces in (middle, last):
        names, pieces, scratch, cost = take(pieces)
        logits, gauss, peak, part = call(
            functools.partial(more_kernel, names),
            (block, block, small(RB), small(RB)),
            in_specs=[VM] * (5 + len(pieces)),
            out_specs=(VM,) * 4,
            scratch=scratch,
            input_output_aliases={0: 0, 1: 1, 2: 2, 3: 3},
            cost_estimate=cost,
        )(in_vmem(logits), in_vmem(gauss), peak, part, in_vmem(panel), *pieces)

    gauss, row_scale, col_shift, part = call(
        first_col_kernel,
        (block, small(RB), small(CB), small(CB)),
        in_specs=[VM] * 5,
        out_specs=(VM,) * 4,
        scratch=[pltpu.VMEM((RB, LANES), F32)],
        input_output_aliases={1: 0},
    )(in_vmem(logits), in_vmem(gauss), over_asset(part), weight, peak)
    part, col_scale = call(first_row_kernel, (small(RB), small(CB)), in_specs=[VM] * 5, out_specs=(VM, VM))(
        in_vmem(gauss), over_slot(part), caps, row_scale, col_shift
    )
    u_space = [pltpu.VMEM((RB, LANES), F32)]
    for iteration in range(1, ITERS - 1):
        part = call(col_kernel, small(CB + SUB), in_specs=[VM] * 5, out_specs=VM, scratch=u_space)(
            in_vmem(gauss), over_asset(part), weight, row_scale, col_scale
        )
        total_parts = over_slot(part)
        part = call(row_kernel, small(RB), in_specs=[VM] * 5, out_specs=VM)(
            in_vmem(gauss), total_parts, caps, row_scale, col_scale
        )
    scaled, part = call(last_col_kernel, (block, small(CB)), in_specs=[VM] * 5, out_specs=(VM, VM), scratch=u_space)(
        in_vmem(gauss), over_asset(part), weight, row_scale, col_scale
    )
    return call(
        plan_kernel,
        jax.ShapeDtypeStruct((ROWS, COLS), F32),
        in_specs=[VM] * 5,
        out_specs=pl.BlockSpec(memory_space=pltpu.HBM),
        scratch=[pltpu.VMEM((ROWS, COLS), F32), pltpu.SemaphoreType.DMA((RB,))],
    )(in_vmem(scaled), over_slot(part), total_parts, caps, col_scale)


def solution(mesh):
    fine = Mesh(mesh.devices.reshape(4, 2, 4, 8), ("y", "c", "x", "z"))
    slot, asset = ("y", "c"), ("x", "z")
    return jax.shard_map(
        per_device,
        mesh=fine,
        in_specs=(P(slot + asset, None), P(slot, asset), P(slot), P(asset)),
        out_specs=P(slot, asset),
        check_vma=False,
    )
```

```python
import functools

import jax
import jax.numpy as jnp
from jax import lax
from jax.experimental import pallas as pl
from jax.experimental.pallas import tpu as pltpu
from jax.sharding import Mesh, PartitionSpec as P

EMB = 768
ITERS = 3
SLOTS = 16384
ASSETS = 32768
ROWS, COLS = 2048, 1024
LANES, SUB = 128, 8
RB, CB = ROWS // LANES, COLS // LANES
VMEM_LIMIT = 28 << 20
F32 = jnp.float32


def shift(value, axis, step):
    size = lax.axis_size(axis)
    return lax.ppermute(value, axis, [(i, (i + step) % size) for i in range(size)])


def ring_gather(value, axis):
    size = lax.axis_size(axis)
    shards = {0: [value]}
    ahead = behind = value
    for step in range(1, size // 2):
        ahead = shift(ahead, axis, 1)
        behind = shift(behind, axis, -1)
        shards[step] = [ahead]
        shards[size - step] = [behind]
    half = value.shape[0] // 2
    shards[size // 2] = [shift(ahead[:half], axis, 1), shift(behind[half:], axis, -1)]
    return shards


def over_asset(part):
    copies = jnp.broadcast_to(part[None], (32,) + part.shape)
    return lax.all_to_all(copies, ("x", "z"), 0, 0, tiled=True)


def over_slot(part):
    copies = jnp.broadcast_to(part[None], (8,) + part.shape)
    return lax.all_to_all(copies, ("y", "c"), 0, 0, tiled=True)


def iotas():
    lane = lax.broadcasted_iota(jnp.int32, (SUB, LANES), 1)
    row = lax.broadcasted_iota(jnp.int32, (SUB, LANES), 0)
    return lane, row


def column(row, g):
    lane, sub = iotas()
    return jnp.sum(jnp.where(lane == sub + SUB * g, row, 0.0), axis=1, keepdims=True)


def place(acc, col, g):
    lane, sub = iotas()
    return jnp.where(lane == sub + SUB * g, col, acc)


def long_row(dense):
    row = jnp.concatenate([dense[k : k + 1, :] for k in range(CB)], axis=1)
    return jnp.broadcast_to(row, (SUB, COLS))


def put_dense(ref, row):
    for k in range(CB):
        ref[k : k + 1, :] = row[:, LANES * k : LANES * (k + 1)]


def fold(wide):
    total = wide[:, :LANES]
    for k in range(1, CB):
        total = total + wide[:, LANES * k : LANES * (k + 1)]
    return total


def log_sum(parts):
    peak = jnp.max(parts, axis=0)
    return peak + jnp.log(jnp.sum(jnp.exp(parts - peak[None]), axis=0))


def groups(b):
    for g in range(LANES // SUB):
        yield g, pl.ds(pl.multiple_of(b * LANES + SUB * g, SUB), SUB)


def row_stats(value, gauss, peak, part, unit):
    peaks = []
    for g in range(LANES // SUB):
        x = value[SUB * g : SUB * (g + 1), :]
        wide = x[:, :LANES]
        for k in range(1, CB):
            wide = jnp.maximum(wide, x[:, LANES * k : LANES * (k + 1)])
        peaks.append(jnp.max(wide, axis=1, keepdims=True))
    peak_row = jnp.zeros((SUB, LANES), F32)
    total_row = jnp.zeros((SUB, LANES), F32)
    for g, at in groups(unit):
        x = jnp.exp(value[SUB * g : SUB * (g + 1), :] - peaks[g])
        gauss[at, :] = x
        total_row = place(total_row, jnp.sum(fold(x), axis=1, keepdims=True), g)
        peak_row = place(peak_row, peaks[g], g)
    peak_row = jnp.sum(peak_row, axis=0, keepdims=True)
    peak[pl.ds(unit, 1), :] = peak_row
    part[pl.ds(unit, 1), :] = peak_row + jnp.log(jnp.sum(total_row, axis=0, keepdims=True))


def block_logits(slot, panel, outs, table, count):
    logits = outs[0]
    for t in range(count // LANES):
        value = jnp.dot(slot[t * LANES : (t + 1) * LANES, :], panel[...], preferred_element_type=F32) * EMB ** (-0.5)
        unit = table[t]
        logits[pl.ds(pl.multiple_of(unit * LANES, LANES), LANES), :] = value
        row_stats(value, *outs[1:], unit)


def back(axis, steps):
    size = lax.axis_size(axis)
    return lax.rem(lax.axis_index(axis) - steps + size, size)


def put_slots(pieces, names, slot, table):
    at = 0
    for ref, (axis, steps, offset) in zip(pieces, names):
        rows = ref.shape[0]
        unit = at // LANES
        if axis == "z":
            table[unit] = back("z", steps)
            for j in range(rows // 32):
                to = pl.multiple_of(unit * LANES + back("x", offset + j) * 32, 32)
                slot[pl.ds(to, 32), :] = ref[32 * j : 32 * (j + 1), :]
        else:
            slot[at : at + rows, :] = ref[...]
            for i in range(rows // LANES):
                table[unit + i] = 8 + 2 * back("x", steps) + offset + i
        at += rows


def reorder_mult(mult):
    value = mult.astype(F32)
    lane, _ = iotas()
    rolled = [value] + [pltpu.roll(value, 32 * k, axis=1) for k in (1, 2, 3)]

    def moved(row, block, to):
        return rolled[(to - block) % 4][row : row + 1, :]

    def merged(pieces):
        out = pieces[0]
        for k in (1, 2, 3):
            out = jnp.where(lane[:1] >= 32 * k, pieces[k], out)
        return out

    rows = [merged([moved(4 * x + z // 2, 2 * (z % 2), x) for x in range(4)]) for z in range(8)]
    for x in range(4):
        for top in range(2):
            rows.append(merged([moved(4 * x + 2 * top + i // 2, 2 * (i % 2) + 1, i) for i in range(4)]))
    return rows


def first_kernel(panel_names, slot_names, *refs):
    n, m = len(panel_names), len(slot_names)
    own, mult, panels, slots = refs[0], refs[1], refs[2 : 2 + n], refs[2 + n : 2 + n + m]
    *outs, panel, weight, slot, table, raw, sems = refs[2 + n + m :]
    at = pl.ds(pl.multiple_of((back("y", 0) * 2 + back("c", 0)) * 96, 32), 96)
    copy = pltpu.make_async_copy(own, panel.at[at], sems.at[0])
    copy.start()
    small_copy = pltpu.make_async_copy(mult, raw, sems.at[1])
    small_copy.start()
    for ref, (y_steps, c_steps) in zip(panels, panel_names):
        start = (back("y", y_steps) * 2 + back("c", c_steps)) * 96
        panel[pl.ds(pl.multiple_of(start, 32), 96), :] = ref[...]
    put_slots(slots, slot_names, slot, table)
    small_copy.wait()
    for i, row in enumerate(reorder_mult(raw[...])):
        weight[i : i + 1, :] = row
    copy.wait()
    block_logits(slot, panel, outs, table, slot.shape[0])


def more_kernel(slot_names, logits, gauss, peak, part, panel, *refs):
    m = len(slot_names)
    del logits, gauss, peak, part
    slots, (*outs, slot, table) = refs[:m], refs[m:]
    put_slots(slots, slot_names, slot, table)
    block_logits(slot, panel, outs, table, slot.shape[0])


def weighted_cols(gauss, weights):
    def block(b, total):
        row = weights[pl.ds(b, 1), :]
        for g, at in groups(b):
            total = total + gauss[at, :] * column(row, g)
        return total

    total = lax.fori_loop(0, RB, block, jnp.zeros((SUB, COLS), F32))
    return jnp.sum(total, axis=0, keepdims=True)


def weighted_rows(gauss, weights, part):
    def block(b, carry):
        acc = jnp.zeros((SUB, LANES), F32)
        for g, at in groups(b):
            acc = place(acc, jnp.sum(fold(gauss[at, :] * weights), axis=1, keepdims=True), g)
        part[pl.ds(b, 1), :] = jnp.sum(acc, axis=0, keepdims=True)
        return carry

    lax.fori_loop(0, RB, block, 0)


def first_col_kernel(logits, before, parts, weight, peak, gauss, row_scale, col_shift, part, pot):
    del before
    pot[...] = jnp.log(weight[...]) - log_sum(parts[...])
    row_scale[...] = jnp.exp(peak[...] + pot[...])
    total = weighted_cols(gauss, row_scale)
    col_shift[...] = jnp.zeros((CB, LANES), F32)
    put_dense(part, jnp.log(total))

    @pl.when(jnp.min(total) < 1e-20)
    def _():
        def shift_block(b, top):
            row = pot[pl.ds(b, 1), :]
            for g, at in groups(b):
                x = logits[at, :] + column(row, g)
                gauss[at, :] = x
                top = jnp.maximum(top, x)
            return top

        top = lax.fori_loop(0, RB, shift_block, jnp.full((SUB, COLS), -jnp.inf, F32))
        top = jnp.max(top, axis=0, keepdims=True)
        wide = jnp.broadcast_to(top, (SUB, COLS))

        def exp_block(b, total):
            for g, at in groups(b):
                x = jnp.exp(gauss[at, :] - wide)
                gauss[at, :] = x
                total = total + x
            return total

        total = lax.fori_loop(0, RB, exp_block, jnp.zeros((SUB, COLS), F32))
        row_scale[...] = jnp.ones((RB, LANES), F32)
        put_dense(col_shift, top)
        put_dense(part, top + jnp.log(jnp.sum(total, axis=0, keepdims=True)))


def first_row_kernel(gauss, parts, caps, row_scale, col_shift, part, col_scale):
    pot = jnp.log(caps[...].astype(F32)) - log_sum(parts[...])
    col_scale[...] = jnp.exp(col_shift[...] + pot)
    weighted_rows(gauss, long_row(col_scale[...]), part)
    part[...] = part[...] * row_scale[...]


def row_kernel(gauss, parts, caps, row_scale, col_scale, part):
    v = caps[...].astype(F32) / jnp.sum(parts[:, :CB], axis=0)
    weighted_rows(gauss, long_row(v * col_scale[...]), part)
    part[...] = part[...] * row_scale[...]


def col_kernel(gauss, parts, weight, row_scale, col_scale, part, u):
    rows = jnp.sum(parts[...], axis=0)
    u[...] = weight[...] / rows * row_scale[...]
    put_dense(part, weighted_cols(gauss, u))
    part[:CB, :] = part[:CB, :] * col_scale[...]
    part[CB:, :] = jnp.broadcast_to(jnp.sum(rows), (SUB, LANES))


def last_col_kernel(gauss, parts, weight, row_scale, col_scale, scaled, part, u):
    u[...] = weight[...] / jnp.sum(parts[...], axis=0) * row_scale[...]

    def block(half):
        def body(b, total):
            row = u[pl.ds(8 * half + b, 1), :]
            for g, at in groups(8 * half + b):
                i, r = g // 4, g % 4
                a = 8 * i + b if half == 0 else 4 * b + i
                value = gauss[at, :] * column(row, g)
                scaled[pl.ds(pl.multiple_of(a * 64 + 32 * half + SUB * r, SUB), SUB), :] = value
                total = total + value
            return total

        return body

    total = lax.fori_loop(0, 8, block(0), jnp.zeros((SUB, COLS), F32))
    total = lax.fori_loop(0, 8, block(1), total)
    put_dense(part, jnp.sum(total, axis=0, keepdims=True))
    part[...] = part[...] * col_scale[...]


def plan_kernel(scaled, parts, total_parts, caps, col_scale, plan, buffer, sems):
    cap_total = jnp.sum(total_parts[:, CB:], axis=0)
    factor = float(SLOTS * ASSETS) / cap_total
    v = long_row(caps[...].astype(F32) / jnp.sum(parts[...], axis=0) * col_scale[...] * factor)

    def copy(b):
        rows = pl.ds(pl.multiple_of(b * LANES, LANES), LANES)
        return pltpu.make_async_copy(buffer.at[rows], plan.at[rows], sems.at[b])

    def block(b, carry):
        for g, at in groups(b):
            buffer[at, :] = scaled[at, :] * v
        copy(b).start()
        return carry

    def wait(b, carry):
        copy(b).wait()
        return carry

    lax.fori_loop(0, RB, block, 0)
    lax.fori_loop(0, RB, wait, 0)


def call(kernel, out_shape, scratch=(), **kwargs):
    return pl.pallas_call(
        kernel,
        out_shape=out_shape,
        scratch_shapes=list(scratch),
        compiler_params=pltpu.CompilerParams(vmem_limit_bytes=VMEM_LIMIT),
        **kwargs,
    )


def in_vmem(value):
    return pltpu.with_memory_space_constraint(value, pltpu.VMEM)


def in_hbm(value):
    return pltpu.with_memory_space_constraint(value, pltpu.HBM)


VM = pl.BlockSpec(memory_space=pltpu.VMEM)


def small(rows):
    return jax.ShapeDtypeStruct((rows, LANES), F32)


def per_device(slot_emb, asset_panel, mult, caps):
    mult = mult.reshape(RB, LANES)
    caps = caps.reshape(CB, LANES)

    panels, panel_names = [shift(asset_panel, "c", 1)], [(0, 1)]
    for steps in (1, 3, 2):
        piece = shift(asset_panel, "y", steps)
        panels += [piece, shift(piece, "c", 1)]
        panel_names += [(steps, 0), (steps, 1)]

    first = [slot_emb[:32]]
    first += [shift(first[0], "x", steps) for steps in (1, 2, 3)]
    first = jnp.concatenate(first)
    ahead, behind = [first], [first]
    for step in range(3):
        ahead.append(shift(ahead[-1], "z", 1))
        behind.append(shift(behind[-1], "z", -1))
    second = jnp.broadcast_to(slot_emb[None, 32:], (8, 32, EMB))
    second = lax.all_to_all(second, "z", 0, 0, tiled=True).reshape(256, EMB)
    second = ring_gather(second, "x")

    block = pltpu.VMEM((ROWS, COLS), F32)

    def take(pieces):
        names = [name for name, piece in pieces]
        pieces = [piece for name, piece in pieces]
        rows = sum(p.shape[0] for p in pieces)
        scratch = [pltpu.VMEM((rows, EMB), jnp.bfloat16), pltpu.SMEM((rows // LANES,), jnp.int32)]
        cost = pl.CostEstimate(flops=2 * rows * EMB * COLS, bytes_accessed=rows * 8192, transcendentals=rows * COLS)
        return names, pieces, scratch, cost

    def some(kind, k):
        if kind == "x":
            return [(("x", k, i), piece) for i, piece in enumerate(second[k])]
        if k == 4:
            return [(("z", 4, 0), shift(ahead[3][:64], "z", 1)), (("z", 4, 2), shift(behind[3][64:], "z", -1))]
        return [(("z", k, 0), ahead[k] if k < 4 else behind[8 - k])]

    names, pieces, scratch, cost = take(sum([some("z", k) for k in (0, 1, 7, 2, 6)], []) + some("x", 0))
    hbm = pl.BlockSpec(memory_space=pltpu.HBM)
    logits, gauss, peak, part, panel, weight = call(
        functools.partial(first_kernel, panel_names, names),
        (block, block, small(RB), small(RB), pltpu.VMEM((EMB, COLS), jnp.bfloat16), small(RB)),
        in_specs=[hbm, hbm] + [VM] * (len(panels) + len(pieces)),
        out_specs=(VM,) * 6,
        scratch=scratch + [pltpu.VMEM((RB, LANES), jnp.int32), pltpu.SemaphoreType.DMA((2,))],
        cost_estimate=cost,
    )(in_hbm(asset_panel), in_hbm(mult), *panels, *pieces)
    ahead[3], behind[3], part = lax.optimization_barrier((ahead[3], behind[3], part))
    middle = some("z", 3) + some("z", 5) + some("x", 1) + some("x", 3) + some("x", 2)
    last = some("z", 4)
    for pieces in (middle, last):
        names, pieces, scratch, cost = take(pieces)
        logits, gauss, peak, part = call(
            functools.partial(more_kernel, names),
            (block, block, small(RB), small(RB)),
            in_specs=[VM] * (5 + len(pieces)),
            out_specs=(VM,) * 4,
            scratch=scratch,
            input_output_aliases={0: 0, 1: 1, 2: 2, 3: 3},
            cost_estimate=cost,
        )(in_vmem(logits), in_vmem(gauss), peak, part, in_vmem(panel), *pieces)

    gauss, row_scale, col_shift, part = call(
        first_col_kernel,
        (block, small(RB), small(CB), small(CB)),
        in_specs=[VM] * 5,
        out_specs=(VM,) * 4,
        scratch=[pltpu.VMEM((RB, LANES), F32)],
        input_output_aliases={1: 0},
    )(in_vmem(logits), in_vmem(gauss), over_asset(part), weight, peak)
    part, col_scale = call(first_row_kernel, (small(RB), small(CB)), in_specs=[VM] * 5, out_specs=(VM, VM))(
        in_vmem(gauss), over_slot(part), caps, row_scale, col_shift
    )
    u_space = [pltpu.VMEM((RB, LANES), F32)]
    for iteration in range(1, ITERS - 1):
        part = call(col_kernel, small(CB + SUB), in_specs=[VM] * 5, out_specs=VM, scratch=u_space)(
            in_vmem(gauss), over_asset(part), weight, row_scale, col_scale
        )
        total_parts = over_slot(part)
        part = call(row_kernel, small(RB), in_specs=[VM] * 5, out_specs=VM)(
            in_vmem(gauss), total_parts, caps, row_scale, col_scale
        )
    scaled, part = call(last_col_kernel, (block, small(CB)), in_specs=[VM] * 5, out_specs=(VM, VM), scratch=u_space)(
        in_vmem(gauss), over_asset(part), weight, row_scale, col_scale
    )
    return call(
        plan_kernel,
        jax.ShapeDtypeStruct((ROWS, COLS), F32),
        in_specs=[VM] * 5,
        out_specs=pl.BlockSpec(memory_space=pltpu.HBM),
        scratch=[pltpu.VMEM((ROWS, COLS), F32), pltpu.SemaphoreType.DMA((RB,))],
    )(in_vmem(scaled), over_slot(part), total_parts, caps, col_scale)


def solution(mesh):
    fine = Mesh(mesh.devices.reshape(4, 2, 4, 8), ("y", "c", "x", "z"))
    slot, asset = ("y", "c"), ("x", "z")
    return jax.shard_map(
        per_device,
        mesh=fine,
        in_specs=(P(slot + asset, None), P(slot, asset), P(slot), P(asset)),
        out_specs=P(slot, asset),
        check_vma=False,
    )
```
